32 devices in a mesh: row: 8 (over z, y), col: 4 (over x, core).
Axes of the slice: x: 2, y: 2, z: 4, core: 2. Of those that a mesh axis runs over, the one named last changes fastest.
Arguments:
- trailing: bfloat16 [12288, 12288], P('row', 'col'), may hold values from -6 to 6
- rows_a: int32 [8, 12], replicated, may hold values from 0 to 11, as said below
- counts_a: int32 [8], replicated, may hold values from 1 to 12, as said below
- factor_a: bfloat16 [12288, 512], P('row'), may hold values from -0.0546875 to 0.0546875
- rows_b: int32 [8, 12], replicated, may hold values from 0 to 11, as said below
- counts_b: int32 [8], replicated, may hold values from 1 to 12, as said below
- factor_b: bfloat16 [12288, 512], P('row'), may hold values from -0.0546875 to 0.0546875
- factor_top: bfloat16 [512, 512], replicated, may hold values from -0.25 to 0.25
- base_a: float32 [512, 512], P('col'), may hold values from -3 to 3
- base_b: float32 [512, 512], P('col'), may hold values from -3 to 3
Outputs:
- column_a: bfloat16 [12288, 512], P('row')
- diag_a: float32 [512, 512], P('col')
- column_b: bfloat16 [12288, 512], P('row')
- top_b: bfloat16 [512, 512], P('col')
- diag_b: float32 [512, 512], P('col')
The draws below stay inside these ranges and needn't reach their ends.
Inputs may be any that keep to these rules, and one draw needn't show every extreme that they name: `rows_a`: the first counts_a[r] entries of row r are distinct; the rest of the row is padding. `counts_a`: some owner uses all 12 slots in every draw. `rows_b`: the first counts_b[r] entries of row r are distinct and lie among the first counts_a[r] entries of row r of rows_a; the rest is padding. counts_b[r] <= counts_a[r]; some owner uses all 12 slots in every draw.
All inputs are finite; a program needn't handle non-finite values.
Results may differ from the reference program's by a relative error of at most 0.007.
Values may be sent and summed in bfloat16 or wider, within the bound.
A program may use at most 128 MiB of HBM per device.

```python
import jax
import jax.numpy as jnp
from jax import lax

BS = 128
W = 512
RBD = 12
PAD = 12
OWNERS = 8
COL_OWNERS = 4
CBD = 24
TRAIL = 12288
SROWS = 12288


def structure(key):
    seeded = jax.random.fold_in(key, 11)
    perm_keys = jax.random.split(jax.random.fold_in(seeded, 1), OWNERS)
    orders = jax.vmap(lambda single: jax.random.permutation(single, RBD))(perm_keys).astype(jnp.int32)
    rows_first = orders[:, :PAD]
    counts = jax.random.randint(jax.random.fold_in(seeded, 2), (OWNERS,), PAD // 2, PAD + 1, dtype=jnp.int32)
    busiest = jax.random.randint(jax.random.fold_in(seeded, 3), (), 0, OWNERS, dtype=jnp.int32)
    lighter = (busiest + 1) % OWNERS
    owners = jnp.arange(OWNERS, dtype=jnp.int32)
    counts_first = jnp.where((owners == busiest) | (owners == lighter), PAD, counts).astype(jnp.int32)
    second = jax.random.randint(jax.random.fold_in(seeded, 4), (OWNERS,), (counts_first + 1) // 2, counts_first + 1, dtype=jnp.int32)
    counts_second = jnp.where(owners == busiest, PAD, second)
    counts_second = jnp.where(owners == lighter, PAD - 1, counts_second).astype(jnp.int32)
    shuffle_keys = jax.random.split(jax.random.fold_in(seeded, 5), OWNERS)
    shuffles = jax.vmap(lambda single: jax.random.permutation(single, PAD))(shuffle_keys).astype(jnp.int32)
    slot_ids = jnp.arange(PAD, dtype=jnp.int32)
    scores = jnp.where(slot_ids[None, :] < counts_first[:, None], shuffles, shuffles + PAD)
    sort_order = jnp.argsort(scores, axis=1, stable=True)
    rows_second = jnp.take_along_axis(rows_first, sort_order, axis=1).astype(jnp.int32)
    return (rows_first, counts_first, rows_second, counts_second)


def draw_rows_a(key, part):
    return structure(key)[0]


def draw_counts_a(key, part):
    return structure(key)[1]


def draw_rows_b(key, part):
    return structure(key)[2]


def draw_counts_b(key, part):
    return structure(key)[3]


def steps_of(rng, dims, pieces, low, largest):
    level = 1.0
    for axis_at, parts in pieces:
        steps = jax.random.uniform(jax.random.fold_in(jax.random.fold_in(rng, 6), axis_at), (parts,), jnp.float32, low / len(pieces), largest / len(pieces))
        level = level * jnp.repeat(jnp.exp(steps), dims[axis_at] // parts).reshape((-1,) + (1,) * (len(dims) - 1 - axis_at))
    return level


def scatter_about(key, shape, deviation, most, cuts=(), kind=jnp.bfloat16):
    loudness = steps_of(key, shape, cuts, -0.22, 0.18) if cuts else 1.0
    drawn = jax.random.normal(key, shape, jnp.float32) * deviation * loudness
    return jnp.minimum(jnp.maximum(drawn, -most), most).astype(kind)


def setup_inputs(seed: int = 0) -> dict:
    keys = jax.random.split(jax.random.key(seed), 11)
    trailing = scatter_about(keys[0], (TRAIL, TRAIL), 1.0, 6.0, ((0, 8), (1, 4)))
    rows_a = draw_rows_a(jax.random.fold_in(keys[10], 71), 0)
    counts_a = draw_counts_a(jax.random.fold_in(keys[10], 71), 0)
    factor_a = scatter_about(keys[3], (SROWS, W), SROWS ** -0.5, 0.0546875, ((0, 8),))
    rows_b = draw_rows_b(jax.random.fold_in(keys[10], 71), 0)
    counts_b = draw_counts_b(jax.random.fold_in(keys[10], 71), 0)
    factor_b = scatter_about(keys[6], (SROWS, W), SROWS ** -0.5, 0.0546875, ((0, 8),))
    factor_top = scatter_about(keys[7], (W, W), W ** -0.5, 0.25)
    base_a = scatter_about(keys[8], (W, W), 0.5, 3.0, ((0, 4),), jnp.float32)
    base_b = scatter_about(keys[9], (W, W), 0.5, 3.0, ((0, 4),), jnp.float32)
    return dict(trailing=trailing, rows_a=rows_a, counts_a=counts_a, factor_a=factor_a, rows_b=rows_b, counts_b=counts_b, factor_b=factor_b, factor_top=factor_top, base_a=base_a, base_b=base_b)


def live_mask(counts):
    slot_ids = jnp.arange(PAD, dtype=jnp.int32)
    return (slot_ids[None, :] < counts[:, None]).astype(jnp.float32)


def block_tiles(trailing, rows):
    owners = jnp.arange(OWNERS, dtype=jnp.int32)
    global_ids = rows * OWNERS + owners[:, None]
    row_pos = (owners[:, None] * RBD + rows).reshape(-1).astype(jnp.int32)
    col_pos = ((global_ids % COL_OWNERS) * CBD + global_ids // COL_OWNERS).reshape(-1).astype(jnp.int32)
    blocks = trailing.reshape(TRAIL // BS, BS, TRAIL // BS, BS)
    picked = jnp.take(blocks, row_pos, axis=0)
    picked = jnp.take(picked, col_pos, axis=2)
    slot_count = OWNERS * PAD
    return picked.reshape(slot_count * BS, slot_count * BS)


def reference(trailing, rows_a, counts_a, factor_a, rows_b, counts_b, factor_b, factor_top, base_a, base_b):
    live_a = live_mask(counts_a)
    live_b = live_mask(counts_b)
    gate_a = jnp.repeat(live_a.reshape(-1), BS)[:, None]
    gate_b = jnp.repeat(live_b.reshape(-1), BS)[:, None]
    tiles_a = block_tiles(trailing, rows_a)
    masked_a = factor_a * gate_a.astype(jnp.bfloat16)
    column_a = (-jnp.dot(tiles_a, masked_a, preferred_element_type=jnp.float32) * gate_a).astype(jnp.bfloat16)
    diag_a = base_a - jnp.dot(column_a.T, factor_a, preferred_element_type=jnp.float32)
    pairing = ((rows_b[:, :, None] == rows_a[:, None, :]) & (live_a[:, None, :] > 0.5) & (live_b[:, :, None] > 0.5)).astype(jnp.float32)
    stacked = column_a.reshape(OWNERS, PAD, BS * W).astype(jnp.float32)
    carried = jnp.einsum("rkq,rqx->rkx", pairing, stacked).reshape(SROWS, W).astype(jnp.bfloat16)
    top_b = (-(jnp.dot(carried.T, factor_b, preferred_element_type=jnp.float32) + jnp.dot(diag_a, factor_top.astype(jnp.float32), precision=lax.Precision.HIGHEST))).astype(jnp.bfloat16)
    tiles_b = block_tiles(trailing, rows_b)
    masked_b = factor_b * gate_b.astype(jnp.bfloat16)
    summed_b = jnp.dot(tiles_b, masked_b, preferred_element_type=jnp.float32) + jnp.dot(carried, factor_top, preferred_element_type=jnp.float32)
    column_b = (-summed_b * gate_b).astype(jnp.bfloat16)
    diag_b = base_b - jnp.dot(column_b.T, factor_b, preferred_element_type=jnp.float32) - jnp.dot(top_b.T, factor_top, preferred_element_type=jnp.float32)
    return column_a, diag_a, column_b, top_b, diag_b
```

```python
import functools

import jax
import jax.numpy as jnp
from jax import lax
from jax.experimental import pallas as pl
from jax.experimental.pallas import tpu as pltpu
from jax.sharding import PartitionSpec as P

MESH = pl.DeviceIdType.MESH
LANES = 128
CORES = 2
SKEW = 1
F32 = jnp.float32
BF16 = jnp.bfloat16


def contract_rows(former, latter):
    return lax.dot_general(
        former, latter, (((0,), (0,)), ((), ())), preferred_element_type=F32
    )


def times_exact(left, right):
    total = None
    for _ in range(3):
        term = left.astype(BF16)
        left = left - term.astype(F32)
        product = jnp.dot(term, right, preferred_element_type=F32)
        total = product if total is None else total + product
    return total


def kept(value, position, count):
    counts = jnp.full((1, value.shape[-1]), count, jnp.int32)
    return value * jnp.where(counts > position, 1.0, 0.0).astype(value.dtype)


class Sizes:
    def __init__(self, rows, cols, trailing, table, factor):
        self.R, self.C = rows, cols
        self.fanout = rows // cols
        self.slots = table[1]
        self.N, self.width = factor
        self.block = self.N // self.slots
        self.mrows, self.mcols = trailing
        self.row_blocks = self.mrows // self.block
        self.X = cols // CORES
        self.Y = self.X
        while rows % self.Y or self.slots % self.Y:
            self.Y -= 1
        self.Z = rows // self.Y
        self.sl = self.slots // self.Y
        self.cw = CORES * LANES
        self.W = self.width // self.cw
        self.chunks = 2 * self.W
        self.T = self.chunks * self.sl
        self.D = SKEW * (self.Z - 1) + 1
        self.pw = self.width // cols
        self.rp = self.pw // rows
        self.tile = self.mrows
        while self.tile > 512:
            self.tile //= 2
        self.G = self.width // LANES


def kernel(n, *refs):
    (
        m_hbm, rows_a, counts_a, fa_hbm, rows_b, counts_b, fb_hbm, ft_hbm, ba_hbm, bb_hbm,
        col_a_out, diag_a_out, col_b_out, top_out, diag_b_out,
        m, fa, fb, ft, ba, bb, held, rhs, acc, own, s1, r1, x2, whole_a, whole_b, fin,
        slot_a, slot_b, part_c, stage, ssend, srecv, agbuf, bsend, brecv, bag,
        diag_a, top, tsend, trecv, tt, diag_b,
        in_sem, m_sem, src_sem, lane_sem, cross_sem, up_sem, down_sem, y_sem, s1_sem,
        core_s, core_r, xs_sem, xr_sem, ws_sem, wr_sem,
        rs_s, rs_r, ag_s, ag_r, t_s, t_r, out_sem,
    ) = refs
    B = n.block
    r, c = lax.axis_index("row"), lax.axis_index("col")
    z, y = r // n.Y, r % n.Y
    x, k = c // CORES, c % CORES
    owners = [c + n.C * i for i in range(n.fanout)]
    z0 = [o // n.Y for o in owners]
    y0 = [o % n.Y for o in owners]
    src = [r == o for o in owners]
    hop = [jnp.abs(z - q) for q in z0]

    def copy_in(a, b, sem):
        cp = pltpu.make_async_copy(a, b, sem)
        cp.start()
        return cp

    def remote(a, b, s, d, dev):
        return pltpu.make_async_remote_copy(
            src_ref=a, dst_ref=b, send_sem=s, recv_sem=d, device_id=dev, device_id_type=MESH
        )

    def wait_recv(ref, sem):
        pltpu.make_async_copy(ref, ref, sem).wait()

    def source_copies(i):
        for w in range(n.chunks):
            whole = (fa_hbm, fb_hbm)[w // n.W]
            yield pltpu.make_async_copy(
                whole.at[:, pl.ds((w % n.W) * n.cw, n.cw)], held.at[w, i], src_sem.at[w]
            )

    for i in range(n.fanout):

        @pl.when(src[i])
        def _():
            for cp in source_copies(i):
                cp.start()

    load_m = [
        copy_in(m_hbm.at[:, j * B : (j + 1) * B], m.at[j], m_sem.at[j])
        for j in range(n.mcols // B)
    ]
    loads = [
        copy_in(a, b, in_sem.at[1 + j])
        for j, (a, b) in enumerate(
            ((fa_hbm, fa), (fb_hbm, fb), (ft_hbm, ft), (ba_hbm, ba), (bb_hbm, bb))
        )
    ]

    def forward(i, t):
        u = t - SKEW * hop[i]

        @pl.when(jnp.logical_and(u >= 0, u < n.T))
        def _():
            w, s = u // n.sl, u % n.sl
            piece = held.at[w, i, pl.ds(pl.multiple_of((y * n.sl + s) * B, B), B)]

            @pl.when(jnp.logical_and(src[i], s == 0))
            def _():
                pltpu.make_async_copy(
                    fa_hbm.at[:, pl.ds(0, n.cw)], held.at[w, i], src_sem.at[w]
                ).wait()

            @pl.when(jnp.logical_not(src[i]))
            def _():
                wait_recv(piece, lane_sem.at[i, u])

            @pl.when(jnp.logical_and(z >= z0[i], z < n.Z - 1))
            def _():
                remote(piece, piece, up_sem.at[i], lane_sem.at[i, u], (r + n.Y, c)).start()

            @pl.when(jnp.logical_and(z <= z0[i], z > 0))
            def _():
                remote(piece, piece, down_sem.at[i], lane_sem.at[i, u], (r - n.Y, c)).start()

            for dy in range(1, n.Y):
                to = lax.rem(y + dy, n.Y)
                dev = (z * n.Y + to, c)

                @pl.when(jnp.logical_not(jnp.logical_and(z == z0[i], to == y0[i])))
                def _():
                    remote(
                        piece, piece, y_sem.at[dy - 1, i], cross_sem.at[n.Y - dy - 1, i, u], dev
                    ).start()

                @pl.when(src[i])
                def _():
                    other = held.at[w, i, pl.ds(pl.multiple_of((to * n.sl + s) * B, B), B)]
                    remote(other, other, s1_sem.at[dy - 1, i], lane_sem.at[i, u], dev).start()

    def product(v):
        w, s = v // n.sl, v % n.sl
        first = w < n.W
        cols = []
        for i in range(n.fanout):
            for dy in range(1, n.Y):

                @pl.when(jnp.logical_not(src[i]))
                def _():
                    lane = lax.rem(y + dy, n.Y)
                    piece = held.at[w, i, pl.ds(pl.multiple_of((lane * n.sl + s) * B, B), B)]
                    wait_recv(piece, cross_sem.at[dy - 1, i, v])

        for i in range(n.fanout):
            count = jnp.where(first, counts_a[owners[i]], counts_b[owners[i]])
            for j in range(n.Y):
                q = j * n.sl + s
                row = jnp.where(first, rows_a[owners[i], q], rows_b[owners[i], q])
                block = held[w, i, pl.ds(pl.multiple_of(q * B, B), B), :]
                rhs[len(cols) * B : (len(cols) + 1) * B, :] = kept(block, q, count)
                cols.append(row * n.fanout + i)

        @pl.loop(0, n.mrows // n.tile)
        def _(step):
            at = pl.ds(pl.multiple_of(step * n.tile, n.tile), n.tile)
            left = jnp.concatenate([m[col, at, :] for col in cols], axis=1)
            part = jnp.dot(left, rhs[...], preferred_element_type=F32)

            @pl.when(s == 0)
            def _():
                acc[at, :] = part

            @pl.when(s != 0)
            def _():
                acc[at, :] += part

    def segment(start, stop):
        def body(t, carry):
            for i in range(n.fanout):
                forward(i, t)
            v = t - n.D

            @pl.when(jnp.logical_and(v >= 0, v < n.T))
            def _():
                product(v)

            return carry

        lax.fori_loop(start, stop, body, 0)

    partner = (r, c + 1 - 2 * k)
    tiles = n.mrows // n.tile

    def row_tiles(f):
        @pl.loop(0, tiles)
        def _(step):
            f(pl.ds(pl.multiple_of(step * n.tile, n.tile), n.tile))

    def core_copy(w):
        return remote(s1.at[w], r1.at[w], core_s.at[w], core_r.at[w], partner)

    def x_copy(w, dx):
        to = lax.rem(x + dx, n.X)
        return remote(
            x2.at[w, x], x2.at[w, x], xs_sem.at[w, dx - 1], xr_sem.at[w, x], (r, to * CORES + k)
        )

    def whole_copy(w):
        whole = (whole_a, whole_b)[w // n.W]
        g = (w % n.W) * CORES + k
        return remote(whole.at[g], whole.at[g], ws_sem.at[w], wr_sem.at[w], partner)

    def reduce_core(w):
        def f(at):
            s1[w, at, :] = acc[at, pl.ds(pl.multiple_of((1 - k) * LANES, LANES), LANES)].astype(BF16)
            own[at, :] = acc[at, pl.ds(pl.multiple_of(k * LANES, LANES), LANES)]

        row_tiles(f)
        core_copy(w).start()

    def reduce_x(w):
        wait_recv(r1.at[w], core_r.at[w])

        def f(at):
            x2[w, x, at, :] = (own[at, :] + r1[w, at, :].astype(F32)).astype(BF16)

        row_tiles(f)
        for dx in range(1, n.X):
            x_copy(w, dx).start()

    def finish(w):
        node = w // n.W
        whole = (whole_a, whole_b)[node]
        for dx in range(1, n.X):
            frm = lax.rem(x + dx, n.X)
            wait_recv(x2.at[w, frm], xr_sem.at[w, frm])
        g = (w % n.W) * CORES + k

        def f(at, some):
            total = x2[w, 0, at, :].astype(F32)
            for j in range(1, n.X):
                total = total + x2[w, j, at, :].astype(F32)
            if node:
                right = ft[:, pl.ds(pl.multiple_of(g * LANES, LANES), LANES)]
                left = jnp.concatenate(
                    [whole_a[j, some].reshape(n.tile, LANES) for j in range(n.G)], axis=1
                )
                total = total + jnp.dot(left, right, preferred_element_type=F32)
            value = (-total).astype(BF16).reshape(n.tile // B, B, LANES)
            whole[g, some] = value
            if node:
                @pl.when(((c * n.pw) // LANES) == g)
                def _():
                    fin[some] = value

        @pl.loop(0, tiles)
        def _(step):
            f(
                pl.ds(pl.multiple_of(step * n.tile, n.tile), n.tile),
                pl.ds(step * (n.tile // B), n.tile // B),
            )

        whole_copy(w).start()

    def gathered(w):
        whole = (whole_a, whole_b)[w // n.W]
        wait_recv(whole.at[(w % n.W) * CORES + 1 - k], wr_sem.at[w])

    def by_slot(dst, whole, rows, counts):
        for q in range(n.slots):
            for g in range(n.G):
                dst[q * B : (q + 1) * B, g * LANES : (g + 1) * LANES] = kept(
                    whole[g, rows[r, q]], q, counts[r]
                )

    group = (c * n.pw) // LANES
    inside = pl.multiple_of(lax.rem(c * n.pw, LANES), n.pw)
    group_at = pl.ds(pl.multiple_of(group * LANES, LANES), LANES)

    def share(send, sem_s, sem_r, recv):
        recv[r] = send[r]
        for dr in range(1, n.R):
            to = lax.rem(r + dr, n.R)
            remote(send.at[to], recv.at[r], sem_s.at[dr - 1], sem_r.at[r], (to, c)).start()

    def add_up(recv, sem_s, sem_r, gather_s, gather_r, bag_ref):
        for dr in range(1, n.R):
            frm = lax.rem(r + dr, n.R)
            wait_recv(recv.at[frm], sem_r.at[frm])
        total = recv[0].astype(F32)
        for j in range(1, n.R):
            total = total + recv[j].astype(F32)
        bag_ref[r] = total.astype(BF16)
        for dr in range(1, n.R):
            to = lax.rem(r + dr, n.R)
            remote(bag_ref.at[r], bag_ref.at[r], gather_s.at[dr - 1], gather_r.at[r], (to, c)).start()

    def gather_sums(bag_ref, gather_r):
        for dr in range(1, n.R):
            frm = lax.rem(r + dr, n.R)
            wait_recv(bag_ref.at[frm], gather_r.at[frm])

    def end_sends(ref_send, sem_s, bag_ref, gather_s):
        for dr in range(1, n.R):
            wait_recv(ref_send.at[0], sem_s.at[dr - 1])
            wait_recv(bag_ref.at[0], gather_s.at[dr - 1])

    def sums_a():
        for cp in loads[:3]:
            cp.wait()
        by_slot(slot_a, whole_a, rows_a, counts_a)
        for q in range(n.slots):
            part_c[q * B : (q + 1) * B, :] = kept(
                whole_a[group, rows_b[r, q]], q, counts_b[r]
            )
        copy_in(slot_a, col_a_out, out_sem.at[0])
        for j, (left, right) in enumerate(((slot_a[:, group_at], fa), (part_c[...], fb))):
            stage[...] = contract_rows(left, right[...])
            mine = stage[pl.ds(inside, n.pw), :]
            for i in range(n.R):
                ssend[i, j] = mine[i * n.rp : (i + 1) * n.rp].astype(BF16)
        share(ssend, rs_s.at[0], rs_r.at[0], srecv)

    def sums_a_add():
        add_up(srecv, rs_s.at[0], rs_r.at[0], ag_s.at[0], ag_r.at[0], agbuf)

    def tops():
        gather_sums(agbuf, ag_r.at[0])
        loads[3].wait()
        sum_a = jnp.concatenate([agbuf[i, 0] for i in range(n.R)], axis=0).astype(F32)
        sum_c = jnp.concatenate([agbuf[i, 1] for i in range(n.R)], axis=0).astype(F32)
        diag_a[...] = ba[...] - sum_a
        top[...] = (-(sum_c + times_exact(diag_a[...], ft[...]))).astype(BF16)
        copy_in(diag_a, diag_a_out, out_sem.at[1])
        copy_in(top, top_out, out_sem.at[2])
        for g in range(n.G):
            tsend[g] = top[:, g * LANES : (g + 1) * LANES]
        trecv[c] = tsend[group]
        for dc in range(1, n.C):
            to = lax.rem(c + dc, n.C)
            remote(
                tsend.at[(to * n.pw) // LANES], trecv.at[c], t_s.at[dc - 1], t_r.at[c], (r, to)
            ).start()

    def tops_in():
        for dc in range(1, n.C):
            frm = lax.rem(c + dc, n.C)
            wait_recv(trecv.at[frm], t_r.at[frm])
        columns = jnp.concatenate([trecv[i] for i in range(n.C)], axis=0)
        tt[...] = contract_rows(columns, ft[...])

    events = {}

    def after(t, f, *args):
        events.setdefault(t, []).append(functools.partial(f, *args))

    end = n.T + n.D
    for w in range(n.chunks):
        done = (w + 1) * n.sl + n.D
        after(done, reduce_core, w)
        if w < n.chunks - 1:
            after(min(done + 1, end), reduce_x, w)
            after(min(done + 5, end), finish, w)
            after(min(done + 6, end), gathered, w)
    ready = n.W * n.sl + n.D + 6
    after(min(ready, end), sums_a)
    after(min(ready + 2, end), sums_a_add)
    after(min(ready + 4, end), tops)
    after(min(ready + 6, end), tops_in)
    at = 0
    for t in sorted(set(events) | {n.D, end}):
        if t > at:
            segment(at, t)
            at = t
        if t == n.D:
            for cp in load_m:
                cp.wait()
        for f in events.get(t, ()):
            f()
    last = n.chunks - 1
    reduce_x(last)
    finish(last)
    if n.pw != LANES:
        gathered(last)
    for q in range(n.slots):
        row = rows_b[r, q]
        value = fin[row] if n.pw == LANES else whole_b[group, row]
        part_c[q * B : (q + 1) * B, :] = kept(value, q, counts_b[r])
    stage[...] = contract_rows(part_c[...], fb[...])
    mine = stage[pl.ds(inside, n.pw), :]
    for i in range(n.R):
        bsend[i] = mine[i * n.rp : (i + 1) * n.rp].astype(BF16)
    share(bsend, rs_s.at[1], rs_r.at[1], brecv)
    if n.pw == LANES:
        gathered(last)
    by_slot(slot_b, whole_b, rows_b, counts_b)
    copy_in(slot_b, col_b_out, out_sem.at[3])
    add_up(brecv, rs_s.at[1], rs_r.at[1], ag_s.at[1], ag_r.at[1], bag)
    for i in range(n.fanout):
        share_of = held.at[:, i, pl.ds(0, n.sl * B)]

        @pl.when(jnp.logical_and(z >= z0[i], z < n.Z - 1))
        def _():
            wait_recv(share_of, up_sem.at[i])

        @pl.when(jnp.logical_and(z <= z0[i], z > 0))
        def _():
            wait_recv(share_of, down_sem.at[i])

        for dy in range(1, n.Y):
            to = lax.rem(y + dy, n.Y)

            @pl.when(jnp.logical_not(jnp.logical_and(z == z0[i], to == y0[i])))
            def _():
                wait_recv(share_of, y_sem.at[dy - 1, i])

            @pl.when(src[i])
            def _():
                wait_recv(share_of, s1_sem.at[dy - 1, i])

    for w in range(n.chunks):
        wait_recv(s1.at[w], core_s.at[w])
        wait_recv(s1.at[w], ws_sem.at[w])
        for dx in range(1, n.X):
            wait_recv(s1.at[w], xs_sem.at[w, dx - 1])
    for dc in range(1, n.C):
        wait_recv(tsend.at[0], t_s.at[dc - 1])
    loads[4].wait()
    gather_sums(bag, ag_r.at[1])
    sum_b = jnp.concatenate([bag[i] for i in range(n.R)], axis=0).astype(F32)
    diag_b[...] = bb[...] - sum_b - tt[pl.ds(inside, n.pw), :]
    copy_in(diag_b, diag_b_out, out_sem.at[4])
    end_sends(ssend, rs_s.at[0], agbuf, ag_s.at[0])
    end_sends(bsend, rs_s.at[1], bag, ag_s.at[1])
    for j, (a, b) in enumerate(
        (
            (slot_a, col_a_out),
            (diag_a, diag_a_out),
            (top, top_out),
            (slot_b, col_b_out),
            (diag_b, diag_b_out),
        )
    ):
        pltpu.make_async_copy(a, b, out_sem.at[j]).wait()


def solution(mesh):
    R, C = mesh.shape["row"], mesh.shape["col"]

    def on_device(trailing, rows_a, counts_a, factor_a, rows_b, counts_b, factor_b, factor_top, base_a, base_b):
        n = Sizes(R, C, trailing.shape, rows_a.shape, factor_a.shape)
        any_ = pl.BlockSpec(memory_space=pl.ANY)
        smem = pl.BlockSpec(memory_space=pltpu.SMEM)
        vm = pltpu.VMEM
        half = (n.mrows, LANES)
        blocks = (n.row_blocks, n.block, LANES)
        dma = pltpu.SemaphoreType.DMA
        shape = jax.ShapeDtypeStruct
        scratch = [
            vm((n.mcols // n.block, n.mrows, n.block), BF16),
            vm(factor_a.shape, BF16),
            vm(factor_b.shape, BF16),
            vm(factor_top.shape, BF16),
            vm(base_a.shape, F32),
            vm(base_b.shape, F32),
            vm((n.chunks, n.fanout, n.N, n.cw), BF16),
            vm((n.fanout * n.Y * n.block, n.cw), BF16),
            vm((n.mrows, n.cw), F32),
            vm(half, F32),
            vm((n.chunks,) + half, BF16),
            vm((n.chunks,) + half, BF16),
            vm((n.chunks, n.X) + half, BF16),
            vm((n.G,) + blocks, BF16),
            vm((n.G,) + blocks, BF16),
            vm(blocks, BF16),
            vm(factor_a.shape, BF16),
            vm(factor_b.shape, BF16),
            vm((n.N, LANES), BF16),
            vm((LANES, n.width), F32),
            vm((n.R, 2, n.rp, n.width), BF16),
            vm((n.R, 2, n.rp, n.width), BF16),
            vm((n.R, 2, n.rp, n.width), BF16),
            vm((n.R, n.rp, n.width), BF16),
            vm((n.R, n.rp, n.width), BF16),
            vm((n.R, n.rp, n.width), BF16),
            vm((n.pw, n.width), F32),
            vm((n.pw, n.width), BF16),
            vm((n.G, n.pw, LANES), BF16),
            vm((n.C, n.pw, LANES), BF16),
            vm((LANES, n.width), F32),
            vm((n.pw, n.width), F32),
            dma((6,)),
            dma((n.mcols // n.block,)),
            dma((n.chunks,)),
            dma((n.fanout, n.T)),
            dma((n.Y - 1, n.fanout, n.T)),
            dma((n.fanout,)),
            dma((n.fanout,)),
            dma((n.Y - 1, n.fanout)),
            dma((n.Y - 1, n.fanout)),
            dma((n.chunks,)),
            dma((n.chunks,)),
            dma((n.chunks, n.X - 1)),
            dma((n.chunks, n.X)),
            dma((n.chunks,)),
            dma((n.chunks,)),
            dma((2, n.R - 1)),
            dma((2, n.R)),
            dma((2, n.R - 1)),
            dma((2, n.R)),
            dma((n.C - 1,)),
            dma((n.C,)),
            dma((5,)),
        ]
        return pl.pallas_call(
            functools.partial(kernel, n),
            out_shape=(
                shape(factor_a.shape, BF16),
                shape((n.pw, n.width), F32),
                shape(factor_b.shape, BF16),
                shape((n.pw, n.width), BF16),
                shape((n.pw, n.width), F32),
            ),
            in_specs=[any_, smem, smem, any_, smem, smem, any_, any_, any_, any_],
            out_specs=(any_,) * 5,
            scratch_shapes=scratch,
            compiler_params=pltpu.CompilerParams(
                has_side_effects=True, vmem_limit_bytes=60 << 20
            ),
        )(trailing, rows_a, counts_a, factor_a, rows_b, counts_b, factor_b, factor_top, base_a, base_b)

    in_specs = (
        P("row", "col"),
        P(),
        P(),
        P("row", None),
        P(),
        P(),
        P("row", None),
        P(),
        P("col", None),
        P("col", None),
    )
    out_specs = (P("row", None), P("col", None), P("row", None), P("col", None), P("col", None))
    return jax.shard_map(
        on_device, mesh=mesh, in_specs=in_specs, out_specs=out_specs, check_vma=False
    )
```

```python
import functools

import jax
import jax.numpy as jnp
from jax import lax
from jax.experimental import pallas as pl
from jax.experimental.pallas import tpu as pltpu
from jax.sharding import PartitionSpec as P

MESH = pl.DeviceIdType.MESH
LANES = 128
CORES = 2
PARTS = 2
SKEW = 3
CROSS = 4
AHEAD = 4
F32 = jnp.float32
BF16 = jnp.bfloat16


def contract_rows(former, latter):
    return lax.dot_general(
        former, latter, (((0,), (0,)), ((), ())), preferred_element_type=F32
    )


def times_exact(left, right):
    total = None
    for _ in range(3):
        term = left.astype(BF16)
        left = left - term.astype(F32)
        product = jnp.dot(term, right, preferred_element_type=F32)
        total = product if total is None else total + product
    return total


def kept(value, position, count):
    counts = jnp.full((1, value.shape[-1]), count, jnp.int32)
    return value * jnp.where(counts > position, 1.0, 0.0).astype(value.dtype)


class Sizes:
    def __init__(self, rows, cols, trailing, table, factor):
        self.R, self.C = rows, cols
        self.fanout = rows // cols
        self.slots = table[1]
        self.N, self.width = factor
        self.block = self.N // self.slots
        self.mrows, self.mcols = trailing
        self.row_blocks = self.mrows // self.block
        self.X = cols // CORES
        self.Y = self.X
        while rows % self.Y or self.slots % self.Y:
            self.Y -= 1
        self.Z = rows // self.Y
        self.sl = self.slots // self.Y
        self.cw = CORES * LANES
        self.W = self.width // self.cw
        self.chunks = 2 * self.W
        self.per = self.sl * PARTS
        self.T = self.chunks * self.per
        self.piece = self.block // PARTS
        self.D = SKEW * (self.Z - 1) + CROSS
        self.pw = self.width // cols
        self.rp = self.pw // rows
        self.tile = self.mrows
        while self.tile > 512:
            self.tile //= 2
        self.G = self.width // LANES
        self.H = self.cw // LANES
        self.half = self.mrows // CORES
        self.half_blocks = self.row_blocks // CORES
        self.htile = self.half // 2

    def group(self, w, h):
        g = w % self.W + self.W * h
        return g, g * LANES // (self.pw * CORES)


def kernel(n, *refs):
    (
        m_hbm, rows_a, counts_a, fa_hbm, rows_b, counts_b, fb_hbm, ft_hbm, ba_hbm, bb_hbm,
        col_a_out, diag_a_out, col_b_out, top_out, diag_b_out,
        m, fa, fb, ft, ba, bb, held, rhs, acc, own, s1, r1, x2s, x2r, whole_a, whole_b, fin,
        slot_a, slot_b, part_a, part_c, stage, ssend, srecv, agbuf, bsend, brecv, bag,
        diag_a, top, tsend, trecv, tt, diag_b,
        in_sem, m_sem, src_sem, lane_sem, cross_sem, up_sem, down_sem, y_sem, s1_sem,
        core_s, core_r, xs_sem, xr_sem, xo_s, xo_r, ws_sem, wr_sem, fin_s, fin_r,
        rs_s, rs_r, ag_s, ag_r, t_s, t_r, out_sem,
    ) = refs
    B = n.block
    r, c = lax.axis_index("row"), lax.axis_index("col")
    z, y = r // n.Y, r % n.Y
    x, k = c // CORES, c % CORES
    owners = [c + n.C * i for i in range(n.fanout)]
    z0 = [o // n.Y for o in owners]
    y0 = [o % n.Y for o in owners]
    src = [r == o for o in owners]
    hop = [jnp.abs(z - q) for q in z0]

    def copy_in(a, b, sem):
        cp = pltpu.make_async_copy(a, b, sem)
        cp.start()
        return cp

    def remote(a, b, s, d, dev):
        return pltpu.make_async_remote_copy(
            src_ref=a, dst_ref=b, send_sem=s, recv_sem=d, device_id=dev, device_id_type=MESH
        )

    def wait_recv(ref, sem):
        pltpu.make_async_copy(ref, ref, sem).wait()

    def source_copies(i):
        for w in range(n.chunks):
            whole = (fa_hbm, fb_hbm)[w // n.W]
            for j in range(n.Y):
                for h in range(n.H):
                    yield pltpu.make_async_copy(
                        whole.at[pl.ds(j * n.per, n.per), :, pl.ds(n.group(w, h)[0] * LANES, LANES)],
                        held.at[i, j, pl.ds(w * n.per, n.per), :, pl.ds(h * LANES, LANES)],
                        src_sem.at[w, j, h],
                    )

    for i in range(n.fanout):

        @pl.when(src[i])
        def _():
            for cp in source_copies(i):
                cp.start()

    load_m = [
        copy_in(m_hbm.at[:, j * B : (j + 1) * B], m.at[j], m_sem.at[j])
        for j in range(n.mcols // B)
    ]
    loads = [
        copy_in(a, b, in_sem.at[1 + j])
        for j, (a, b) in enumerate(
            ((fa_hbm, fa), (fb_hbm, fb), (ft_hbm, ft), (ba_hbm, ba), (bb_hbm, bb))
        )
    ]

    def to_lane(i, u):
        for dy in range(1, n.Y):
            to = lax.rem(y + dy, n.Y)
            other = held.at[i, to, u]
            dev = (z * n.Y + to, c)
            remote(other, other, s1_sem.at[dy - 1, i], lane_sem.at[i, u], dev).start()

    barrier = pltpu.get_barrier_semaphore()
    peers = [(lax.rem(r + dr, n.R), c) for dr in range(1, n.R)]
    peers += [(r, lax.rem(c + dc, n.C)) for dc in range(1, n.C)]
    for dev in peers:
        pl.semaphore_signal(barrier, inc=1, device_id=dev, device_id_type=MESH)
    pl.semaphore_wait(barrier, len(peers))
    for i in range(n.fanout):

        @pl.when(src[i])
        def _():
            for cp in source_copies(i):
                cp.wait()
            for u in range(AHEAD):
                to_lane(i, u)

    def forward(i, t):
        u = t - SKEW * hop[i]

        @pl.when(jnp.logical_and(u >= 0, u < n.T))
        def _():
            piece = held.at[i, y, u]

            @pl.when(src[i])
            def _():
                later = u + AHEAD

                @pl.when(later < n.T)
                def _():
                    to_lane(i, later)

            @pl.when(jnp.logical_not(src[i]))
            def _():
                wait_recv(piece, lane_sem.at[i, u])

            @pl.when(jnp.logical_and(z >= z0[i], z < n.Z - 1))
            def _():
                remote(piece, piece, up_sem.at[i], lane_sem.at[i, u], (r + n.Y, c)).start()

            @pl.when(jnp.logical_and(z <= z0[i], z > 0))
            def _():
                remote(piece, piece, down_sem.at[i], lane_sem.at[i, u], (r - n.Y, c)).start()

            for dy in range(1, n.Y):
                to = lax.rem(y + dy, n.Y)

                @pl.when(jnp.logical_not(jnp.logical_and(z == z0[i], to == y0[i])))
                def _():
                    remote(
                        piece,
                        piece,
                        y_sem.at[dy - 1, i],
                        cross_sem.at[n.Y - dy - 1, i, u],
                        (z * n.Y + to, c),
                    ).start()

    def product(v):
        s = lax.rem(v, n.sl)
        first = v < n.W * n.sl
        cols = []
        for i in range(n.fanout):
            for dy in range(1, n.Y):

                @pl.when(jnp.logical_not(src[i]))
                def _():
                    for h in range(PARTS):
                        u = v * PARTS + h
                        wait_recv(held.at[i, lax.rem(y + dy, n.Y), u], cross_sem.at[dy - 1, i, u])

        for i in range(n.fanout):
            count = jnp.where(first, counts_a[owners[i]], counts_b[owners[i]])
            for j in range(n.Y):
                q = j * n.sl + s
                row = jnp.where(first, rows_a[owners[i], q], rows_b[owners[i], q])
                block = held[i, j, pl.ds(v * PARTS, PARTS)].reshape(B, n.cw)
                rhs[len(cols) * B : (len(cols) + 1) * B, :] = kept(block, q, count)
                cols.append(row * n.fanout + i)

        @pl.loop(0, n.mrows // n.tile)
        def _(step):
            at = pl.ds(pl.multiple_of(step * n.tile, n.tile), n.tile)
            left = jnp.concatenate([m[col, at, :] for col in cols], axis=1)
            part = jnp.dot(left, rhs[...], preferred_element_type=F32)

            @pl.when(s == 0)
            def _():
                acc[at, :] = part

            @pl.when(s != 0)
            def _():
                acc[at, :] += part

    def segment(start, stop):
        def body(t, carry):
            for i in range(n.fanout):
                forward(i, t)
            late = t - n.D + 1

            @pl.when(jnp.logical_and(late > 0, lax.rem(late, PARTS) == 0))
            def _():
                product(lax.div(late, PARTS) - 1)

            return carry

        lax.fori_loop(start, stop, body, 0)

    partner = (r, c + 1 - 2 * k)

    mine_rows = pl.ds(pl.multiple_of(k * n.half, n.half), n.half)
    mine_blocks = pl.ds(k * n.half_blocks, n.half_blocks)
    other_blocks = pl.ds((1 - k) * n.half_blocks, n.half_blocks)
    wholes = (whole_a, whole_b)

    def half_tiles(f):
        @pl.loop(0, n.half // n.htile)
        def _(step):
            f(pl.multiple_of(step * n.htile, n.htile))

    def at_owner(w, f, g=None):
        for h in range(n.H):
            index, chip = n.group(w, h)
            if f is not None:

                @pl.when(x == chip)
                def _():
                    f(h, index)

            if g is not None:

                @pl.when(x != chip)
                def _():
                    g(h, index)

    def reduce_core(w):
        def f(at):
            theirs = pl.ds(pl.multiple_of((1 - k) * n.half + at, n.htile), n.htile)
            ours = pl.ds(pl.multiple_of(k * n.half + at, n.htile), n.htile)
            s1[w, pl.ds(at, n.htile), :] = acc[theirs, :].astype(BF16)
            own[pl.ds(at, n.htile), :] = acc[ours, :]

        half_tiles(f)
        remote(s1.at[w], r1.at[w], core_s.at[w], core_r.at[w], partner).start()

    def reduce_x(w):
        wait_recv(r1.at[w], core_r.at[w])

        def f(at):
            rows = pl.ds(at, n.htile)
            total = own[rows, :] + r1[w, rows, :].astype(F32)
            own[rows, :] = total
            for h in range(n.H):
                x2s[w, h, rows, :] = total[:, h * LANES : (h + 1) * LANES].astype(BF16)

        half_tiles(f)

        def send(h, g):
            chip = n.group(w, h)[1]
            remote(
                x2s.at[w, h], x2r.at[w, h, x], xs_sem.at[w, h], xr_sem.at[w, h, x], (r, chip * CORES + k)
            ).start()

        at_owner(w, None, send)

    def to_partner(w, h, g):
        part = wholes[w // n.W].at[g, mine_blocks]
        remote(part, part, ws_sem.at[w, h], wr_sem.at[w, h], partner).start()

    def finish(w):
        node = w // n.W

        def own_group(h, g):
            for dx in range(1, n.X):
                frm = lax.rem(x + dx, n.X)
                wait_recv(x2r.at[w, h, frm], xr_sem.at[w, h, frm])

            def f(at):
                rows = pl.ds(at, n.htile)
                count = n.htile // B
                some = pl.ds(k * n.half_blocks + lax.div(at, B), count)
                total = own[rows, h * LANES : (h + 1) * LANES]
                for dx in range(1, n.X):
                    total = total + x2r[w, h, lax.rem(x + dx, n.X), rows, :].astype(F32)
                if node:
                    left = jnp.concatenate(
                        [whole_a[j, some].reshape(n.htile, LANES) for j in range(n.G)], axis=1
                    )
                    right = ft[:, g * LANES : (g + 1) * LANES]
                    total = total + jnp.dot(left, right, preferred_element_type=F32)
                value = (-total).astype(BF16).reshape(count, B, LANES)
                wholes[node][g, some] = value
                if node:
                    fin[w % n.W, some] = value

            half_tiles(f)
            if node:
                part = fin.at[w % n.W, mine_blocks]
                remote(part, part, fin_s.at[w % n.W], fin_r.at[w % n.W], partner).start()
            part = wholes[node].at[g, mine_blocks]
            for dx in range(1, n.X):
                to = lax.rem(x + dx, n.X)
                remote(
                    part, part, xo_s.at[w, h, dx - 1], xo_r.at[w, h], (r, to * CORES + k)
                ).start()
            to_partner(w, h, g)

        at_owner(w, own_group)

    def relay(w):
        def f(h, g):
            wait_recv(wholes[w // n.W].at[g, mine_blocks], xo_r.at[w, h])
            to_partner(w, h, g)

        at_owner(w, None, f)

    def gathered(w):
        for h in range(n.H):
            g = n.group(w, h)[0]
            wait_recv(wholes[w // n.W].at[g, other_blocks], wr_sem.at[w, h])

    def fins():
        for w in range(n.W):

            def f(h, g):
                wait_recv(fin.at[w, other_blocks], fin_r.at[w])

            at_owner(w, f)

    def by_slot(dst, whole, rows, counts):
        for q in range(n.slots):
            for g in range(n.G):
                dst[q * B : (q + 1) * B, g * LANES : (g + 1) * LANES] = kept(
                    whole[g, rows[r, q]], q, counts[r]
                )

    group = (c * n.pw) // LANES
    inside = pl.multiple_of(lax.rem(c * n.pw, LANES), n.pw)

    def share(send, sem_s, sem_r, recv):
        recv[r] = send[r]
        for dr in range(1, n.R):
            to = lax.rem(r + dr, n.R)
            remote(send.at[to], recv.at[r], sem_s.at[dr - 1], sem_r.at[r], (to, c)).start()

    def add_up(recv, sem_s, sem_r, gather_s, gather_r, bag_ref):
        for dr in range(1, n.R):
            frm = lax.rem(r + dr, n.R)
            wait_recv(recv.at[frm], sem_r.at[frm])
        total = recv[0].astype(F32)
        for j in range(1, n.R):
            total = total + recv[j].astype(F32)
        bag_ref[r] = total.astype(BF16)
        for dr in range(1, n.R):
            to = lax.rem(r + dr, n.R)
            remote(bag_ref.at[r], bag_ref.at[r], gather_s.at[dr - 1], gather_r.at[r], (to, c)).start()

    def gather_sums(bag_ref, gather_r):
        for dr in range(1, n.R):
            frm = lax.rem(r + dr, n.R)
            wait_recv(bag_ref.at[frm], gather_r.at[frm])

    def end_sends(ref_send, sem_s, bag_ref, gather_s):
        for dr in range(1, n.R):
            wait_recv(ref_send.at[0], sem_s.at[dr - 1])
            wait_recv(bag_ref.at[0], gather_s.at[dr - 1])

    def sums_a():
        for cp in loads[:3]:
            cp.wait()
        for q in range(n.slots):
            at = slice(q * B, (q + 1) * B)
            part_a[at, :] = kept(whole_a[group, rows_a[r, q]], q, counts_a[r])
            part_c[at, :] = kept(whole_a[group, rows_b[r, q]], q, counts_b[r])
        for j, (left, right) in enumerate(((part_a[...], fa), (part_c[...], fb))):
            stage[...] = contract_rows(left, right[...].reshape(n.N, n.width))
            mine = stage[pl.ds(inside, n.pw), :]
            for i in range(n.R):
                ssend[i, j] = mine[i * n.rp : (i + 1) * n.rp].astype(BF16)
        share(ssend, rs_s.at[0], rs_r.at[0], srecv)

    def sums_a_add():
        add_up(srecv, rs_s.at[0], rs_r.at[0], ag_s.at[0], ag_r.at[0], agbuf)

    def tops():
        gather_sums(agbuf, ag_r.at[0])
        loads[3].wait()
        sum_a = jnp.concatenate([agbuf[i, 0] for i in range(n.R)], axis=0).astype(F32)
        sum_c = jnp.concatenate([agbuf[i, 1] for i in range(n.R)], axis=0).astype(F32)
        diag_a[...] = ba[...] - sum_a
        top[...] = (-(sum_c + times_exact(diag_a[...], ft[...]))).astype(BF16)
        copy_in(diag_a, diag_a_out, out_sem.at[1])
        copy_in(top, top_out, out_sem.at[2])
        for g in range(n.G):
            tsend[g] = top[:, g * LANES : (g + 1) * LANES]
        trecv[c] = tsend[group]
        for dc in range(1, n.C):
            to = lax.rem(c + dc, n.C)
            remote(
                tsend.at[(to * n.pw) // LANES], trecv.at[c], t_s.at[dc - 1], t_r.at[c], (r, to)
            ).start()

    def tops_in():
        for dc in range(1, n.C):
            frm = lax.rem(c + dc, n.C)
            wait_recv(trecv.at[frm], t_r.at[frm])
        columns = jnp.concatenate([trecv[i] for i in range(n.C)], axis=0)
        tt[...] = contract_rows(columns, ft[...])

    events = {}

    def after(t, f, *args):
        events.setdefault(min(t, end), []).append(functools.partial(f, *args))

    end = n.T + n.D
    last = n.chunks - 1
    for w in range(last):
        done = (w + 1) * n.per + n.D
        after(done, reduce_core, w)
        after(done + 1 * PARTS, reduce_x, w)
        after(done + 4 * PARTS, finish, w)
        if w < last - 1:
            after(done + 7 * PARTS, relay, w)
            after(done + 8 * PARTS, gathered, w)
    after(n.W * n.per + n.D + 8 * PARTS, sums_a)
    at = 0
    for t in sorted(set(events) | {n.D, end}):
        if t > at:
            segment(at, t)
            at = t
        if t == n.D:
            for cp in load_m:
                cp.wait()
        for f in events.get(t, ()):
            f()
    reduce_core(last)
    relay(last - 1)
    sums_a_add()
    reduce_x(last)
    tops()
    by_slot(slot_a, whole_a, rows_a, counts_a)
    copy_in(slot_a, col_a_out, out_sem.at[0])
    finish(last)
    fins()
    for q in range(n.slots):
        part_c[q * B : (q + 1) * B, :] = kept(
            fin[lax.rem(group, n.W), rows_b[r, q]], q, counts_b[r]
        )
    stage[...] = contract_rows(part_c[...], fb[...].reshape(n.N, n.width))
    mine = stage[pl.ds(inside, n.pw), :]
    for i in range(n.R):
        bsend[i] = mine[i * n.rp : (i + 1) * n.rp].astype(BF16)
    share(bsend, rs_s.at[1], rs_r.at[1], brecv)
    tops_in()
    gathered(last - 1)
    relay(last)
    add_up(brecv, rs_s.at[1], rs_r.at[1], ag_s.at[1], ag_r.at[1], bag)
    gathered(last)
    by_slot(slot_b, whole_b, rows_b, counts_b)
    copy_in(slot_b, col_b_out, out_sem.at[3])
    for i in range(n.fanout):
        share_of = held.at[i, 0]

        @pl.when(jnp.logical_and(z >= z0[i], z < n.Z - 1))
        def _():
            wait_recv(share_of, up_sem.at[i])

        @pl.when(jnp.logical_and(z <= z0[i], z > 0))
        def _():
            wait_recv(share_of, down_sem.at[i])

        for dy in range(1, n.Y):
            to = lax.rem(y + dy, n.Y)

            @pl.when(jnp.logical_not(jnp.logical_and(z == z0[i], to == y0[i])))
            def _():
                wait_recv(share_of, y_sem.at[dy - 1, i])

            @pl.when(src[i])
            def _():
                wait_recv(share_of, s1_sem.at[dy - 1, i])

    for w in range(n.chunks):
        wait_recv(s1.at[w], core_s.at[w])

        def sent(h, g):
            for dx in range(1, n.X):
                wait_recv(x2s.at[w, h], xo_s.at[w, h, dx - 1])
            if w >= n.W:
                wait_recv(x2s.at[w, h], fin_s.at[w % n.W])

        def sent_part(h, g):
            wait_recv(x2s.at[w, h], xs_sem.at[w, h])

        at_owner(w, sent, sent_part)
        for h in range(n.H):
            wait_recv(x2s.at[w, h], ws_sem.at[w, h])
    for dc in range(1, n.C):
        wait_recv(tsend.at[0], t_s.at[dc - 1])
    loads[4].wait()
    gather_sums(bag, ag_r.at[1])
    sum_b = jnp.concatenate([bag[i] for i in range(n.R)], axis=0).astype(F32)
    diag_b[...] = bb[...] - sum_b - tt[pl.ds(inside, n.pw), :]
    copy_in(diag_b, diag_b_out, out_sem.at[4])
    end_sends(ssend, rs_s.at[0], agbuf, ag_s.at[0])
    end_sends(bsend, rs_s.at[1], bag, ag_s.at[1])
    for j, (a, b) in enumerate(
        (
            (slot_a, col_a_out),
            (diag_a, diag_a_out),
            (top, top_out),
            (slot_b, col_b_out),
            (diag_b, diag_b_out),
        )
    ):
        pltpu.make_async_copy(a, b, out_sem.at[j]).wait()


def solution(mesh):
    R, C = mesh.shape["row"], mesh.shape["col"]

    def on_device(trailing, rows_a, counts_a, factor_a, rows_b, counts_b, factor_b, factor_top, base_a, base_b):
        n = Sizes(R, C, trailing.shape, rows_a.shape, factor_a.shape)
        any_ = pl.BlockSpec(memory_space=pl.ANY)
        smem = pl.BlockSpec(memory_space=pltpu.SMEM)
        vm = pltpu.VMEM
        blocks = (n.row_blocks, n.block, LANES)
        dma = pltpu.SemaphoreType.DMA
        shape = jax.ShapeDtypeStruct
        scratch = [
            vm((n.mcols // n.block, n.mrows, n.block), BF16),
            vm((n.slots * PARTS, n.piece, n.width), BF16),
            vm((n.slots * PARTS, n.piece, n.width), BF16),
            vm(factor_top.shape, BF16),
            vm(base_a.shape, F32),
            vm(base_b.shape, F32),
            vm((n.fanout, n.Y, n.T, n.piece, n.cw), BF16),
            vm((n.fanout * n.Y * n.block, n.cw), BF16),
            vm((n.mrows, n.cw), F32),
            vm((n.half, n.cw), F32),
            vm((n.chunks, n.half, n.cw), BF16),
            vm((n.chunks, n.half, n.cw), BF16),
            vm((n.chunks, n.H, n.half, LANES), BF16),
            vm((n.chunks, n.H, n.X, n.half, LANES), BF16),
            vm((n.G,) + blocks, BF16),
            vm((n.G,) + blocks, BF16),
            vm((n.W,) + blocks, BF16),
            vm(factor_a.shape, BF16),
            vm(factor_b.shape, BF16),
            vm((n.N, LANES), BF16),
            vm((n.N, LANES), BF16),
            vm((LANES, n.width), F32),
            vm((n.R, 2, n.rp, n.width), BF16),
            vm((n.R, 2, n.rp, n.width), BF16),
            vm((n.R, 2, n.rp, n.width), BF16),
            vm((n.R, n.rp, n.width), BF16),
            vm((n.R, n.rp, n.width), BF16),
            vm((n.R, n.rp, n.width), BF16),
            vm((n.pw, n.width), F32),
            vm((n.pw, n.width), BF16),
            vm((n.G, n.pw, LANES), BF16),
            vm((n.C, n.pw, LANES), BF16),
            vm((LANES, n.width), F32),
            vm((n.pw, n.width), F32),
            dma((6,)),
            dma((n.mcols // n.block,)),
            dma((n.chunks, n.Y, n.H)),
            dma((n.fanout, n.T)),
            dma((n.Y - 1, n.fanout, n.T)),
            dma((n.fanout,)),
            dma((n.fanout,)),
            dma((n.Y - 1, n.fanout)),
            dma((n.Y - 1, n.fanout)),
            dma((n.chunks,)),
            dma((n.chunks,)),
            dma((n.chunks, n.H)),
            dma((n.chunks, n.H, n.X)),
            dma((n.chunks, n.H, n.X - 1)),
            dma((n.chunks, n.H)),
            dma((n.chunks, n.H)),
            dma((n.chunks, n.H)),
            dma((n.W,)),
            dma((n.W,)),
            dma((2, n.R - 1)),
            dma((2, n.R)),
            dma((2, n.R - 1)),
            dma((2, n.R)),
            dma((n.C - 1,)),
            dma((n.C,)),
            dma((5,)),
        ]
        return pl.pallas_call(
            functools.partial(kernel, n),
            out_shape=(
                shape(factor_a.shape, BF16),
                shape((n.pw, n.width), F32),
                shape(factor_b.shape, BF16),
                shape((n.pw, n.width), BF16),
                shape((n.pw, n.width), F32),
            ),
            in_specs=[any_, smem, smem, any_, smem, smem, any_, any_, any_, any_],
            out_specs=(any_,) * 5,
            scratch_shapes=scratch,
            compiler_params=pltpu.CompilerParams(
                collective_id=0, has_side_effects=True, vmem_limit_bytes=60 << 20
            ),
        )(
            trailing,
            rows_a,
            counts_a,
            factor_a.reshape(n.slots * PARTS, n.piece, n.width),
            rows_b,
            counts_b,
            factor_b.reshape(n.slots * PARTS, n.piece, n.width),
            factor_top,
            base_a,
            base_b,
        )

    in_specs = (
        P("row", "col"),
        P(),
        P(),
        P("row", None),
        P(),
        P(),
        P("row", None),
        P(),
        P("col", None),
        P("col", None),
    )
    out_specs = (P("row", None), P("col", None), P("row", None), P("col", None), P("col", None))
    return jax.shard_map(
        on_device, mesh=mesh, in_specs=in_specs, out_specs=out_specs, check_vma=False
    )
```

```python
import functools

import jax
import jax.numpy as jnp
from jax import lax
from jax.experimental import pallas as pl
from jax.experimental.pallas import tpu as pltpu
from jax.sharding import PartitionSpec as P

MESH = pl.DeviceIdType.MESH
LANES = 128
CORES = 2
PARTS = 1
SKEW = 3
CROSS = 3
F32 = jnp.float32
BF16 = jnp.bfloat16


def contract_rows(former, latter):
    return lax.dot_general(
        former, latter, (((0,), (0,)), ((), ())), preferred_element_type=F32
    )


def times_exact(left, right):
    total = None
    for _ in range(3):
        term = left.astype(BF16)
        left = left - term.astype(F32)
        product = jnp.dot(term, right, preferred_element_type=F32)
        total = product if total is None else total + product
    return total


def kept(value, position, count):
    counts = jnp.full((1, value.shape[-1]), count, jnp.int32)
    return value * jnp.where(counts > position, 1.0, 0.0).astype(value.dtype)


class Sizes:
    def __init__(self, rows, cols, trailing, table, factor):
        self.R, self.C = rows, cols
        self.fanout = rows // cols
        self.slots = table[1]
        self.N, self.width = factor
        self.block = self.N // self.slots
        self.mrows, self.mcols = trailing
        self.row_blocks = self.mrows // self.block
        self.X = cols // CORES
        self.Y = self.X
        while rows % self.Y:
            self.Y -= 1
        self.Z = rows // self.Y
        self.deep = 2 - self.slots % 2
        self.cw = CORES * LANES
        self.W = self.width // self.cw
        self.chunks = 2 * self.W
        self.per = self.slots * PARTS
        self.Q = self.deep * PARTS
        self.T = self.chunks * self.per
        self.piece = self.block // PARTS
        self.D = SKEW * (self.Z - 1) + CROSS
        self.pw = self.width // cols
        self.rp = self.pw // rows
        self.tile = self.mrows
        while self.tile > 512:
            self.tile //= 2
        self.G = self.width // LANES
        self.H = self.cw // LANES
        self.half = self.mrows // CORES
        self.half_blocks = self.row_blocks // CORES
        self.htile = self.half // 2

    def group(self, w, h):
        g = w % self.W + self.W * h
        return g, g * LANES // (self.pw * CORES)


def kernel(n, *refs):
    (
        m_hbm, rows_a, counts_a, fa_hbm, rows_b, counts_b, fb_hbm, ft_hbm, ba_hbm, bb_hbm,
        col_a_out, diag_a_out, col_b_out, top_out, diag_b_out,
        m, fa, fb, ft, ba, bb, held, rhs, acc, own, s1, r1, x2s, x2r, whole_a, whole_b, fin,
        slot_a, slot_b, part_a, part_c, stage, ssend, srecv, agbuf, bsend, brecv, bag,
        diag_a, top, tsend, trecv, tt, diag_b,
        in_sem, m_sem, src_sem, lane_sem, up_sem, down_sem, y_sem,
        core_s, core_r, xs_sem, xr_sem, xo_s, xo_r, ws_sem, wr_sem, fin_s, fin_r,
        rs_s, rs_r, ag_s, ag_r, t_s, t_r, out_sem,
    ) = refs
    B = n.block
    r, c = lax.axis_index("row"), lax.axis_index("col")
    z, y = r // n.Y, r % n.Y
    x, k = c // CORES, c % CORES
    owners = [c + n.C * i for i in range(n.fanout)]
    z0 = [o // n.Y for o in owners]
    y0 = [o % n.Y for o in owners]
    src = [r == o for o in owners]
    hop = [jnp.abs(z - q) for q in z0]

    def copy_in(a, b, sem):
        cp = pltpu.make_async_copy(a, b, sem)
        cp.start()
        return cp

    def remote(a, b, s, d, dev):
        return pltpu.make_async_remote_copy(
            src_ref=a, dst_ref=b, send_sem=s, recv_sem=d, device_id=dev, device_id_type=MESH
        )

    def wait_recv(ref, sem):
        pltpu.make_async_copy(ref, ref, sem).wait()

    def source_copies(i):
        for w in range(n.chunks):
            whole = (fa_hbm, fb_hbm)[w // n.W]
            for h in range(n.H):
                yield pltpu.make_async_copy(
                    whole.at[:, :, pl.ds(n.group(w, h)[0] * LANES, LANES)],
                    held.at[i, pl.ds(w * n.per, n.per), :, pl.ds(h * LANES, LANES)],
                    src_sem.at[w, h],
                )

    for i in range(n.fanout):

        @pl.when(src[i])
        def _():
            for cp in source_copies(i):
                cp.start()

    load_m = [
        copy_in(m_hbm.at[:, j * B : (j + 1) * B], m.at[j], m_sem.at[j])
        for j in range(n.mcols // B)
    ]
    loads = [
        copy_in(a, b, in_sem.at[1 + j])
        for j, (a, b) in enumerate(
            ((fa_hbm, fa), (fb_hbm, fb), (ft_hbm, ft), (ba_hbm, ba), (bb_hbm, bb))
        )
    ]

    barrier = pltpu.get_barrier_semaphore()
    peers = [(lax.rem(r + dr, n.R), c) for dr in range(1, n.R)]
    peers += [(r, lax.rem(c + dc, n.C)) for dc in range(1, n.C)]
    for dev in peers:
        pl.semaphore_signal(barrier, inc=1, device_id=dev, device_id_type=MESH)
    pl.semaphore_wait(barrier, len(peers))
    for i in range(n.fanout):

        @pl.when(src[i])
        def _():
            for cp in source_copies(i):
                cp.wait()

    trunk = [y == q for q in y0]

    def forward(i, t):
        u = t - SKEW * hop[i]

        @pl.when(jnp.logical_and(trunk[i], jnp.logical_and(u >= 0, u < n.T)))
        def _():
            piece = held.at[i, u]

            @pl.when(jnp.logical_not(src[i]))
            def _():
                wait_recv(piece, lane_sem.at[i, u])

            @pl.when(jnp.logical_and(z >= z0[i], z < n.Z - 1))
            def _():
                remote(piece, piece, up_sem.at[i], lane_sem.at[i, u], (r + n.Y, c)).start()

            @pl.when(jnp.logical_and(z <= z0[i], z > 0))
            def _():
                remote(piece, piece, down_sem.at[i], lane_sem.at[i, u], (r - n.Y, c)).start()

            for dy in range(1, n.Y):
                dev = (z * n.Y + lax.rem(y + dy, n.Y), c)
                remote(piece, piece, y_sem.at[dy - 1, i], lane_sem.at[i, u], dev).start()

    def product(v):
        s = lax.rem(v, n.slots // n.deep)
        first = v < n.W * (n.slots // n.deep)
        cols = []
        for i in range(n.fanout):

            @pl.when(jnp.logical_not(trunk[i]))
            def _():
                for h in range(n.Q):
                    u = v * n.Q + h
                    wait_recv(held.at[i, u], lane_sem.at[i, u])

        for i in range(n.fanout):
            count = jnp.where(first, counts_a[owners[i]], counts_b[owners[i]])
            for j in range(n.deep):
                q = s * n.deep + j
                row = jnp.where(first, rows_a[owners[i], q], rows_b[owners[i], q])
                block = held[i, pl.ds(v * n.Q + j * PARTS, PARTS)].reshape(B, n.cw)
                rhs[len(cols) * B : (len(cols) + 1) * B, :] = kept(block, q, count)
                cols.append(row * n.fanout + i)

        @pl.loop(0, n.mrows // n.tile)
        def _(step):
            at = pl.ds(pl.multiple_of(step * n.tile, n.tile), n.tile)
            left = jnp.concatenate([m[col, at, :] for col in cols], axis=1)
            part = jnp.dot(left, rhs[...], preferred_element_type=F32)

            @pl.when(s == 0)
            def _():
                acc[at, :] = part

            @pl.when(s != 0)
            def _():
                acc[at, :] += part

    def segment(start, stop):
        def body(t, carry):
            for i in range(n.fanout):
                forward(i, t)
            late = t - n.D + 1

            @pl.when(jnp.logical_and(late > 0, lax.rem(late, n.Q) == 0))
            def _():
                product(lax.div(late, n.Q) - 1)

            return carry

        lax.fori_loop(start, stop, body, 0)

    partner = (r, c + 1 - 2 * k)

    mine_rows = pl.ds(pl.multiple_of(k * n.half, n.half), n.half)
    mine_blocks = pl.ds(k * n.half_blocks, n.half_blocks)
    other_blocks = pl.ds((1 - k) * n.half_blocks, n.half_blocks)
    wholes = (whole_a, whole_b)

    def half_tiles(f):
        @pl.loop(0, n.half // n.htile)
        def _(step):
            f(pl.multiple_of(step * n.htile, n.htile))

    def at_owner(w, f, g=None):
        for h in range(n.H):
            index, chip = n.group(w, h)
            if f is not None:

                @pl.when(x == chip)
                def _():
                    f(h, index)

            if g is not None:

                @pl.when(x != chip)
                def _():
                    g(h, index)

    def reduce_core(w):
        def f(at):
            theirs = pl.ds(pl.multiple_of((1 - k) * n.half + at, n.htile), n.htile)
            ours = pl.ds(pl.multiple_of(k * n.half + at, n.htile), n.htile)
            s1[w, pl.ds(at, n.htile), :] = acc[theirs, :].astype(BF16)
            own[pl.ds(at, n.htile), :] = acc[ours, :]

        half_tiles(f)
        remote(s1.at[w], r1.at[w], core_s.at[w], core_r.at[w], partner).start()

    def reduce_x(w):
        wait_recv(r1.at[w], core_r.at[w])

        def f(at):
            rows = pl.ds(at, n.htile)
            total = own[rows, :] + r1[w, rows, :].astype(F32)
            own[rows, :] = total
            for h in range(n.H):
                x2s[w, h, rows, :] = total[:, h * LANES : (h + 1) * LANES].astype(BF16)

        half_tiles(f)

        def send(h, g):
            chip = n.group(w, h)[1]
            remote(
                x2s.at[w, h], x2r.at[w, h, x], xs_sem.at[w, h], xr_sem.at[w, h, x], (r, chip * CORES + k)
            ).start()

        at_owner(w, None, send)

    def to_partner(w, h, g):
        part = wholes[w // n.W].at[g, mine_blocks]
        remote(part, part, ws_sem.at[w, h], wr_sem.at[w, h], partner).start()

    def finish(w):
        node = w // n.W

        def own_group(h, g):
            for dx in range(1, n.X):
                frm = lax.rem(x + dx, n.X)
                wait_recv(x2r.at[w, h, frm], xr_sem.at[w, h, frm])

            def f(at):
                rows = pl.ds(at, n.htile)
                count = n.htile // B
                some = pl.ds(k * n.half_blocks + lax.div(at, B), count)
                total = own[rows, h * LANES : (h + 1) * LANES]
                for dx in range(1, n.X):
                    total = total + x2r[w, h, lax.rem(x + dx, n.X), rows, :].astype(F32)
                if node:
                    left = jnp.concatenate(
                        [whole_a[j, some].reshape(n.htile, LANES) for j in range(n.G)], axis=1
                    )
                    right = ft[:, g * LANES : (g + 1) * LANES]
                    total = total + jnp.dot(left, right, preferred_element_type=F32)
                value = (-total).astype(BF16).reshape(count, B, LANES)
                wholes[node][g, some] = value
                if node:
                    fin[w % n.W, some] = value

            half_tiles(f)
            if node:
                part = fin.at[w % n.W, mine_blocks]
                remote(part, part, fin_s.at[w % n.W], fin_r.at[w % n.W], partner).start()
            part = wholes[node].at[g, mine_blocks]
            for dx in range(1, n.X):
                to = lax.rem(x + dx, n.X)
                remote(
                    part, part, xo_s.at[w, h, dx - 1], xo_r.at[w, h], (r, to * CORES + k)
                ).start()
            to_partner(w, h, g)

        at_owner(w, own_group)

    def relay(w):
        def f(h, g):
            wait_recv(wholes[w // n.W].at[g, mine_blocks], xo_r.at[w, h])
            to_partner(w, h, g)

        at_owner(w, None, f)

    def gathered(w):
        for h in range(n.H):
            g = n.group(w, h)[0]
            wait_recv(wholes[w // n.W].at[g, other_blocks], wr_sem.at[w, h])

    def fins():
        for w in range(n.W):

            def f(h, g):
                wait_recv(fin.at[w, other_blocks], fin_r.at[w])

            at_owner(w, f)

    def by_slot(dst, whole, rows, counts):
        for q in range(n.slots):
            for g in range(n.G):
                dst[q * B : (q + 1) * B, g * LANES : (g + 1) * LANES] = kept(
                    whole[g, rows[r, q]], q, counts[r]
                )

    group = (c * n.pw) // LANES
    inside = pl.multiple_of(lax.rem(c * n.pw, LANES), n.pw)

    def share(send, sem_s, sem_r, recv):
        recv[r] = send[r]
        for dr in range(1, n.R):
            to = lax.rem(r + dr, n.R)
            remote(send.at[to], recv.at[r], sem_s.at[dr - 1], sem_r.at[r], (to, c)).start()

    def add_up(recv, sem_s, sem_r, gather_s, gather_r, bag_ref):
        for dr in range(1, n.R):
            frm = lax.rem(r + dr, n.R)
            wait_recv(recv.at[frm], sem_r.at[frm])
        total = recv[0].astype(F32)
        for j in range(1, n.R):
            total = total + recv[j].astype(F32)
        bag_ref[r] = total.astype(BF16)
        for dr in range(1, n.R):
            to = lax.rem(r + dr, n.R)
            remote(bag_ref.at[r], bag_ref.at[r], gather_s.at[dr - 1], gather_r.at[r], (to, c)).start()

    def gather_sums(bag_ref, gather_r):
        for dr in range(1, n.R):
            frm = lax.rem(r + dr, n.R)
            wait_recv(bag_ref.at[frm], gather_r.at[frm])

    def end_sends(ref_send, sem_s, bag_ref, gather_s):
        for dr in range(1, n.R):
            wait_recv(ref_send.at[0], sem_s.at[dr - 1])
            wait_recv(bag_ref.at[0], gather_s.at[dr - 1])

    def sums_a():
        for cp in loads[:3]:
            cp.wait()
        for q in range(n.slots):
            at = slice(q * B, (q + 1) * B)
            part_a[at, :] = kept(whole_a[group, rows_a[r, q]], q, counts_a[r])
            part_c[at, :] = kept(whole_a[group, rows_b[r, q]], q, counts_b[r])
        for j, (left, right) in enumerate(((part_a[...], fa), (part_c[...], fb))):
            stage[...] = contract_rows(left, right[...].reshape(n.N, n.width))
            mine = stage[pl.ds(inside, n.pw), :]
            for i in range(n.R):
                ssend[i, j] = mine[i * n.rp : (i + 1) * n.rp].astype(BF16)
        share(ssend, rs_s.at[0], rs_r.at[0], srecv)

    def sums_a_add():
        add_up(srecv, rs_s.at[0], rs_r.at[0], ag_s.at[0], ag_r.at[0], agbuf)

    def tops():
        gather_sums(agbuf, ag_r.at[0])
        loads[3].wait()
        sum_a = jnp.concatenate([agbuf[i, 0] for i in range(n.R)], axis=0).astype(F32)
        sum_c = jnp.concatenate([agbuf[i, 1] for i in range(n.R)], axis=0).astype(F32)
        diag_a[...] = ba[...] - sum_a
        top[...] = (-(sum_c + times_exact(diag_a[...], ft[...]))).astype(BF16)
        copy_in(diag_a, diag_a_out, out_sem.at[1])
        copy_in(top, top_out, out_sem.at[2])
        for g in range(n.G):
            tsend[g] = top[:, g * LANES : (g + 1) * LANES]
        trecv[c] = tsend[group]
        for dc in range(1, n.C):
            to = lax.rem(c + dc, n.C)
            remote(
                tsend.at[(to * n.pw) // LANES], trecv.at[c], t_s.at[dc - 1], t_r.at[c], (r, to)
            ).start()

    def tops_in():
        for dc in range(1, n.C):
            frm = lax.rem(c + dc, n.C)
            wait_recv(trecv.at[frm], t_r.at[frm])
        columns = jnp.concatenate([trecv[i] for i in range(n.C)], axis=0)
        tt[...] = contract_rows(columns, ft[...])

    events = {}

    def after(t, f, *args):
        events.setdefault(min(t, end), []).append(functools.partial(f, *args))

    end = n.T + n.D
    last = n.chunks - 1
    for w in range(last):
        done = (w + 1) * n.per + n.D
        after(done, reduce_core, w)
        after(done + 1 * n.Q, reduce_x, w)
        after(done + 4 * n.Q, finish, w)
        if w < last - 1:
            after(done + 7 * n.Q, relay, w)
            after(done + 8 * n.Q, gathered, w)
    after(n.W * n.per + n.D + 8 * n.Q, sums_a)
    at = 0
    for t in sorted(set(events) | {n.D, end}):
        if t > at:
            segment(at, t)
            at = t
        if t == n.D:
            for cp in load_m:
                cp.wait()
        for f in events.get(t, ()):
            f()
    reduce_core(last)
    relay(last - 1)
    sums_a_add()
    reduce_x(last)
    tops()
    by_slot(slot_a, whole_a, rows_a, counts_a)
    copy_in(slot_a, col_a_out, out_sem.at[0])
    finish(last)
    fins()
    for q in range(n.slots):
        part_c[q * B : (q + 1) * B, :] = kept(
            fin[lax.rem(group, n.W), rows_b[r, q]], q, counts_b[r]
        )
    stage[...] = contract_rows(part_c[...], fb[...].reshape(n.N, n.width))
    mine = stage[pl.ds(inside, n.pw), :]
    for i in range(n.R):
        bsend[i] = mine[i * n.rp : (i + 1) * n.rp].astype(BF16)
    share(bsend, rs_s.at[1], rs_r.at[1], brecv)
    tops_in()
    gathered(last - 1)
    relay(last)
    add_up(brecv, rs_s.at[1], rs_r.at[1], ag_s.at[1], ag_r.at[1], bag)
    gathered(last)
    by_slot(slot_b, whole_b, rows_b, counts_b)
    copy_in(slot_b, col_b_out, out_sem.at[3])
    for i in range(n.fanout):
        share_of = held.at[i]

        @pl.when(jnp.logical_and(trunk[i], jnp.logical_and(z >= z0[i], z < n.Z - 1)))
        def _():
            wait_recv(share_of, up_sem.at[i])

        @pl.when(jnp.logical_and(trunk[i], jnp.logical_and(z <= z0[i], z > 0)))
        def _():
            wait_recv(share_of, down_sem.at[i])

        @pl.when(trunk[i])
        def _():
            for dy in range(1, n.Y):
                wait_recv(share_of, y_sem.at[dy - 1, i])

    for w in range(n.chunks):
        wait_recv(s1.at[w], core_s.at[w])

        def sent(h, g):
            for dx in range(1, n.X):
                wait_recv(x2s.at[w, h], xo_s.at[w, h, dx - 1])
            if w >= n.W:
                wait_recv(x2s.at[w, h], fin_s.at[w % n.W])

        def sent_part(h, g):
            wait_recv(x2s.at[w, h], xs_sem.at[w, h])

        at_owner(w, sent, sent_part)
        for h in range(n.H):
            wait_recv(x2s.at[w, h], ws_sem.at[w, h])
    for dc in range(1, n.C):
        wait_recv(tsend.at[0], t_s.at[dc - 1])
    loads[4].wait()
    gather_sums(bag, ag_r.at[1])
    sum_b = jnp.concatenate([bag[i] for i in range(n.R)], axis=0).astype(F32)
    diag_b[...] = bb[...] - sum_b - tt[pl.ds(inside, n.pw), :]
    copy_in(diag_b, diag_b_out, out_sem.at[4])
    end_sends(ssend, rs_s.at[0], agbuf, ag_s.at[0])
    end_sends(bsend, rs_s.at[1], bag, ag_s.at[1])
    for j, (a, b) in enumerate(
        (
            (slot_a, col_a_out),
            (diag_a, diag_a_out),
            (top, top_out),
            (slot_b, col_b_out),
            (diag_b, diag_b_out),
        )
    ):
        pltpu.make_async_copy(a, b, out_sem.at[j]).wait()


def hand_over(*refs):
    count = (len(refs) - 2) // 3
    sources, results, held = (refs[j * count : (j + 1) * count] for j in range(3))
    load_sem, store_sem = refs[-2:]
    loads = [
        pltpu.make_async_copy(a, b, load_sem.at[j]) for j, (a, b) in enumerate(zip(sources, held))
    ]
    stores = [
        pltpu.make_async_copy(a, b, store_sem.at[j]) for j, (a, b) in enumerate(zip(held, results))
    ]
    for cp in loads:
        cp.start()
    for load, store in zip(loads, stores):
        load.wait()
        store.start()
    for cp in stores:
        cp.wait()


def handed_over(arrays):
    spec = pl.BlockSpec(memory_space=pl.ANY)
    count = len(arrays)
    return pl.pallas_call(
        hand_over,
        out_shape=tuple(jax.ShapeDtypeStruct(a.shape, a.dtype) for a in arrays),
        in_specs=[spec] * count,
        out_specs=(spec,) * count,
        scratch_shapes=[pltpu.VMEM(a.shape, a.dtype) for a in arrays]
        + [pltpu.SemaphoreType.DMA((count,))] * 2,
        compiler_params=pltpu.CompilerParams(vmem_limit_bytes=60 << 20),
    )(*arrays)


def solution(mesh):
    R, C = mesh.shape["row"], mesh.shape["col"]

    def on_device(trailing, rows_a, counts_a, factor_a, rows_b, counts_b, factor_b, factor_top, base_a, base_b):
        n = Sizes(R, C, trailing.shape, rows_a.shape, factor_a.shape)
        any_ = pl.BlockSpec(memory_space=pl.ANY)
        smem = pl.BlockSpec(memory_space=pltpu.SMEM)
        vm = pltpu.VMEM
        blocks = (n.row_blocks, n.block, LANES)
        dma = pltpu.SemaphoreType.DMA
        shape = jax.ShapeDtypeStruct
        scratch = [
            vm((n.mcols // n.block, n.mrows, n.block), BF16),
            vm((n.slots * PARTS, n.piece, n.width), BF16),
            vm((n.slots * PARTS, n.piece, n.width), BF16),
            vm(factor_top.shape, BF16),
            vm(base_a.shape, F32),
            vm(base_b.shape, F32),
            vm((n.fanout, n.T, n.piece, n.cw), BF16),
            vm((n.fanout * n.deep * n.block, n.cw), BF16),
            vm((n.mrows, n.cw), F32),
            vm((n.half, n.cw), F32),
            vm((n.chunks, n.half, n.cw), BF16),
            vm((n.chunks, n.half, n.cw), BF16),
            vm((n.chunks, n.H, n.half, LANES), BF16),
            vm((n.chunks, n.H, n.X, n.half, LANES), BF16),
            vm((n.G,) + blocks, BF16),
            vm((n.G,) + blocks, BF16),
            vm((n.W,) + blocks, BF16),
            vm(factor_a.shape, BF16),
            vm(factor_b.shape, BF16),
            vm((n.N, LANES), BF16),
            vm((n.N, LANES), BF16),
            vm((LANES, n.width), F32),
            vm((n.R, 2, n.rp, n.width), BF16),
            vm((n.R, 2, n.rp, n.width), BF16),
            vm((n.R, 2, n.rp, n.width), BF16),
            vm((n.R, n.rp, n.width), BF16),
            vm((n.R, n.rp, n.width), BF16),
            vm((n.R, n.rp, n.width), BF16),
            vm((n.pw, n.width), F32),
            vm((n.pw, n.width), BF16),
            vm((n.G, n.pw, LANES), BF16),
            vm((n.C, n.pw, LANES), BF16),
            vm((LANES, n.width), F32),
            vm((n.pw, n.width), F32),
            dma((6,)),
            dma((n.mcols // n.block,)),
            dma((n.chunks, n.H)),
            dma((n.fanout, n.T)),
            dma((n.fanout,)),
            dma((n.fanout,)),
            dma((n.Y - 1, n.fanout)),
            dma((n.chunks,)),
            dma((n.chunks,)),
            dma((n.chunks, n.H)),
            dma((n.chunks, n.H, n.X)),
            dma((n.chunks, n.H, n.X - 1)),
            dma((n.chunks, n.H)),
            dma((n.chunks, n.H)),
            dma((n.chunks, n.H)),
            dma((n.W,)),
            dma((n.W,)),
            dma((2, n.R - 1)),
            dma((2, n.R)),
            dma((2, n.R - 1)),
            dma((2, n.R)),
            dma((n.C - 1,)),
            dma((n.C,)),
            dma((5,)),
        ]
        results = pl.pallas_call(
            functools.partial(kernel, n),
            out_shape=(
                shape(factor_a.shape, BF16),
                shape((n.pw, n.width), F32),
                shape(factor_b.shape, BF16),
                shape((n.pw, n.width), BF16),
                shape((n.pw, n.width), F32),
            ),
            in_specs=[any_, smem, smem, any_, smem, smem, any_, any_, any_, any_],
            out_specs=(any_,) * 5,
            scratch_shapes=scratch,
            compiler_params=pltpu.CompilerParams(
                collective_id=0, has_side_effects=True, vmem_limit_bytes=60 << 20
            ),
        )(
            trailing,
            rows_a,
            counts_a,
            factor_a.reshape(n.slots * PARTS, n.piece, n.width),
            rows_b,
            counts_b,
            factor_b.reshape(n.slots * PARTS, n.piece, n.width),
            factor_top,
            base_a,
            base_b,
        )
        return handed_over(results)

    in_specs = (
        P("row", "col"),
        P(),
        P(),
        P("row", None),
        P(),
        P(),
        P("row", None),
        P(),
        P("col", None),
        P("col", None),
    )
    out_specs = (P("row", None), P("col", None), P("row", None), P("col", None), P("col", None))
    return jax.shard_map(
        on_device, mesh=mesh, in_specs=in_specs, out_specs=out_specs, check_vma=False
    )
```

```python
import functools

import jax
import jax.numpy as jnp
from jax import lax
from jax.experimental import pallas as pl
from jax.experimental.pallas import tpu as pltpu
from jax.sharding import PartitionSpec as P

MESH = pl.DeviceIdType.MESH
LANES = 128
CORES = 2
PARTS = 1
SKEW = 4
CROSS = 3
F32 = jnp.float32
BF16 = jnp.bfloat16


def contract_rows(former, latter):
    return lax.dot_general(
        former, latter, (((0,), (0,)), ((), ())), preferred_element_type=F32
    )


def times_exact(left, right):
    total = None
    for _ in range(3):
        term = left.astype(BF16)
        left = left - term.astype(F32)
        product = jnp.dot(term, right, preferred_element_type=F32)
        total = product if total is None else total + product
    return total


def kept(value, position, count):
    counts = jnp.full((1, value.shape[-1]), count, jnp.int32)
    return value * jnp.where(counts > position, 1.0, 0.0).astype(value.dtype)


class Sizes:
    def __init__(self, rows, cols, trailing, table, factor):
        self.R, self.C = rows, cols
        self.fanout = rows // cols
        self.slots = table[1]
        self.N, self.width = factor
        self.block = self.N // self.slots
        self.mrows, self.mcols = trailing
        self.row_blocks = self.mrows // self.block
        self.X = cols // CORES
        self.Y = self.X
        while rows % self.Y:
            self.Y -= 1
        self.Z = rows // self.Y
        self.deep = 2 - self.slots % 2
        self.cw = CORES * LANES
        self.W = self.width // self.cw
        self.chunks = 2 * self.W
        self.per = self.slots * PARTS
        self.Q = self.deep * PARTS
        self.T = self.chunks * self.per
        self.piece = self.block // PARTS
        self.D = SKEW * (self.Z - 1) + CROSS
        self.pw = self.width // cols
        self.rp = self.pw // rows
        self.tile = self.mrows
        while self.tile > 512:
            self.tile //= 2
        self.G = self.width // LANES
        self.H = self.cw // LANES
        self.half = self.mrows // CORES
        self.half_blocks = self.row_blocks // CORES
        self.htile = self.half // 2

    def group(self, w, h):
        g = w % self.W + self.W * h
        return g, g * LANES // (self.pw * CORES)

    def columns(self, g):
        return [c for c in range(self.C) if c * self.pw // LANES == g]


def kernel(n, *refs):
    (
        m_hbm, rows_a, counts_a, fa_hbm, rows_b, counts_b, fb_hbm, ft_hbm, ba_hbm, bb_hbm,
        col_a_out, diag_a_out, col_b_out, top_out, diag_b_out,
        m, fa, fb, ft, ba, bb, held, rhs, acc, own, s1, r1, x2s, x2r, whole_a, whole_b, chosen,
        slot_a, slot_b, part_a, part_c, stage, ssend, srecv, agbuf, bsend, brecv, bag,
        diag_a, top, tsend, trecv, tt, diag_b,
        in_sem, m_sem, src_sem, lane_sem, up_sem, down_sem, y_sem,
        core_s, core_r, xs_sem, xr_sem, xo_s, xo_r, ws_sem, wr_sem,
        rs_s, rs_r, bs_s, bs_r, ag_s, ag_r, t_s, t_r, out_sem,
    ) = refs
    B = n.block
    r, c = lax.axis_index("row"), lax.axis_index("col")
    z, y = r // n.Y, r % n.Y
    x, k = c // CORES, c % CORES
    owners = [c + n.C * i for i in range(n.fanout)]
    z0 = [o // n.Y for o in owners]
    y0 = [o % n.Y for o in owners]
    src = [r == o for o in owners]
    hop = [jnp.abs(z - q) for q in z0]

    def copy_in(a, b, sem):
        cp = pltpu.make_async_copy(a, b, sem)
        cp.start()
        return cp

    def remote(a, b, s, d, dev):
        return pltpu.make_async_remote_copy(
            src_ref=a, dst_ref=b, send_sem=s, recv_sem=d, device_id=dev, device_id_type=MESH
        )

    def wait_recv(ref, sem):
        pltpu.make_async_copy(ref, ref, sem).wait()

    def source_copies(i):
        for w in range(n.chunks):
            whole = (fa_hbm, fb_hbm)[w // n.W]
            for h in range(n.H):
                yield pltpu.make_async_copy(
                    whole.at[:, :, pl.ds(n.group(w, h)[0] * LANES, LANES)],
                    held.at[i, pl.ds(w * n.per, n.per), :, pl.ds(h * LANES, LANES)],
                    src_sem.at[w, h],
                )

    for i in range(n.fanout):

        @pl.when(src[i])
        def _():
            for cp in source_copies(i):
                cp.start()

    load_m = [
        copy_in(m_hbm.at[:, j * B : (j + 1) * B], m.at[j], m_sem.at[j])
        for j in range(n.mcols // B)
    ]
    loads = [
        copy_in(a, b, in_sem.at[1 + j])
        for j, (a, b) in enumerate(
            ((fa_hbm, fa), (fb_hbm, fb), (ft_hbm, ft), (ba_hbm, ba), (bb_hbm, bb))
        )
    ]

    barrier = pltpu.get_barrier_semaphore()
    peers = [(lax.rem(r + dr, n.R), c) for dr in range(1, n.R)]
    peers += [(r, lax.rem(c + dc, n.C)) for dc in range(1, n.C)]
    for dev in peers:
        pl.semaphore_signal(barrier, inc=1, device_id=dev, device_id_type=MESH)
    pl.semaphore_wait(barrier, len(peers))
    for i in range(n.fanout):

        @pl.when(src[i])
        def _():
            for cp in source_copies(i):
                cp.wait()

    trunk = [y == q for q in y0]

    def forward(i, t):
        u = t - SKEW * hop[i]

        @pl.when(jnp.logical_and(trunk[i], jnp.logical_and(u >= 0, u < n.T)))
        def _():
            piece = held.at[i, u]

            @pl.when(jnp.logical_not(src[i]))
            def _():
                wait_recv(piece, lane_sem.at[i, u])

            @pl.when(jnp.logical_and(z >= z0[i], z < n.Z - 1))
            def _():
                remote(piece, piece, up_sem.at[i], lane_sem.at[i, u], (r + n.Y, c)).start()

            @pl.when(jnp.logical_and(z <= z0[i], z > 0))
            def _():
                remote(piece, piece, down_sem.at[i], lane_sem.at[i, u], (r - n.Y, c)).start()

            for dy in range(1, n.Y):
                dev = (z * n.Y + lax.rem(y + dy, n.Y), c)
                remote(piece, piece, y_sem.at[dy - 1, i], lane_sem.at[i, u], dev).start()

    def product(v):
        s = lax.rem(v, n.slots // n.deep)
        first = v < n.W * (n.slots // n.deep)
        cols = []
        for i in range(n.fanout):

            @pl.when(jnp.logical_not(trunk[i]))
            def _():
                for h in range(n.Q):
                    u = v * n.Q + h
                    wait_recv(held.at[i, u], lane_sem.at[i, u])

        for i in range(n.fanout):
            count = jnp.where(first, counts_a[owners[i]], counts_b[owners[i]])
            for j in range(n.deep):
                q = s * n.deep + j
                row = jnp.where(first, rows_a[owners[i], q], rows_b[owners[i], q])
                block = held[i, pl.ds(v * n.Q + j * PARTS, PARTS)].reshape(B, n.cw)
                rhs[len(cols) * B : (len(cols) + 1) * B, :] = kept(block, q, count)
                cols.append(row * n.fanout + i)

        @pl.loop(0, n.mrows // n.tile)
        def _(step):
            at = pl.ds(pl.multiple_of(step * n.tile, n.tile), n.tile)
            left = jnp.concatenate([m[col, at, :] for col in cols], axis=1)
            part = jnp.dot(left, rhs[...], preferred_element_type=F32)

            @pl.when(s == 0)
            def _():
                acc[at, :] = part

            @pl.when(s != 0)
            def _():
                acc[at, :] += part

    def segment(start, stop):
        def body(t, carry):
            for i in range(n.fanout):
                forward(i, t)
            late = t - n.D + 1

            @pl.when(jnp.logical_and(late > 0, lax.rem(late, n.Q) == 0))
            def _():
                product(lax.div(late, n.Q) - 1)

            return carry

        lax.fori_loop(start, stop, body, 0)

    partner = (r, c + 1 - 2 * k)

    mine_rows = pl.ds(pl.multiple_of(k * n.half, n.half), n.half)
    mine_blocks = pl.ds(k * n.half_blocks, n.half_blocks)
    other_blocks = pl.ds((1 - k) * n.half_blocks, n.half_blocks)
    wholes = (whole_a, whole_b)

    def half_tiles(f):
        @pl.loop(0, n.half // n.htile)
        def _(step):
            f(pl.multiple_of(step * n.htile, n.htile))

    def at_owner(w, f, g=None):
        for h in range(n.H):
            index, chip = n.group(w, h)
            if f is not None:

                @pl.when(x == chip)
                def _():
                    f(h, index)

            if g is not None:

                @pl.when(x != chip)
                def _():
                    g(h, index)

    def reduce_core(w):
        def f(at):
            theirs = pl.ds(pl.multiple_of((1 - k) * n.half + at, n.htile), n.htile)
            ours = pl.ds(pl.multiple_of(k * n.half + at, n.htile), n.htile)
            s1[w, pl.ds(at, n.htile), :] = acc[theirs, :].astype(BF16)
            own[pl.ds(at, n.htile), :] = acc[ours, :]

        half_tiles(f)
        remote(s1.at[w], r1.at[w], core_s.at[w], core_r.at[w], partner).start()

    def reduce_x(w):
        wait_recv(r1.at[w], core_r.at[w])

        def f(at):
            rows = pl.ds(at, n.htile)
            total = own[rows, :] + r1[w, rows, :].astype(F32)
            own[rows, :] = total
            for h in range(n.H):
                x2s[w, h, rows, :] = total[:, h * LANES : (h + 1) * LANES].astype(BF16)

        half_tiles(f)

        def send(h, g):
            chip = n.group(w, h)[1]
            remote(
                x2s.at[w, h], x2r.at[w, h, x], xs_sem.at[w, h], xr_sem.at[w, h, x], (r, chip * CORES + k)
            ).start()

        at_owner(w, None, send)

    def to_partner(w, h, g):
        part = wholes[w // n.W].at[g, mine_blocks]
        remote(part, part, ws_sem.at[w, h], wr_sem.at[w, h], partner).start()

    def finish(w):
        node = w // n.W

        def own_group(h, g):
            for dx in range(1, n.X):
                frm = lax.rem(x + dx, n.X)
                wait_recv(x2r.at[w, h, frm], xr_sem.at[w, h, frm])

            def f(at):
                rows = pl.ds(at, n.htile)
                count = n.htile // B
                some = pl.ds(k * n.half_blocks + lax.div(at, B), count)
                total = own[rows, h * LANES : (h + 1) * LANES]
                for dx in range(1, n.X):
                    total = total + x2r[w, h, lax.rem(x + dx, n.X), rows, :].astype(F32)
                if node:
                    left = jnp.concatenate(
                        [whole_a[j, some].reshape(n.htile, LANES) for j in range(n.G)], axis=1
                    )
                    right = ft[:, g * LANES : (g + 1) * LANES]
                    total = total + jnp.dot(left, right, preferred_element_type=F32)
                value = (-total).astype(BF16).reshape(count, B, LANES)
                wholes[node][g, some] = value

            half_tiles(f)
            part = wholes[node].at[g, mine_blocks]
            for dx in range(1, n.X):
                to = lax.rem(x + dx, n.X)
                remote(
                    part, part, xo_s.at[w, h, dx - 1], xo_r.at[w, h], (r, to * CORES + k)
                ).start()
            to_partner(w, h, g)
            if node:
                sums_b(w % n.W, g)

        at_owner(w, own_group)

    def to_owners(turn, c_to):
        kd = c_to % CORES
        for dr in range(n.R):
            to = lax.rem(r + dr, n.R)
            copy = remote(
                bsend.at[turn, kd, to], brecv.at[r, k], bs_s.at[turn, kd, dr], bs_r.at[r, k], (to, c_to)
            )
            yield dr, kd, to, copy

    def sums_b(turn, g):
        left = whole_b[g, mine_blocks].reshape(n.half, LANES)
        sums = contract_rows(left, chosen[...])
        for c_to in n.columns(g):
            inside = c_to * n.pw - g * LANES
            kd = c_to % CORES
            for i in range(n.R):
                at = inside + i * n.rp
                bsend[turn, kd, i] = sums[at : at + n.rp].astype(BF16)
            for dr, kd, to, copy in to_owners(turn, c_to):
                if dr:
                    copy.start()
                else:
                    pl.when(k != kd)(copy.start)

                    @pl.when(k == kd)
                    def _():
                        brecv[r, k] = bsend[turn, kd, to]

    def choose():
        for cp in loads[:3]:
            cp.wait()
        for b in range(n.half_blocks):
            slot, live = 0, 0
            for q in range(n.slots):
                hit = (rows_b[r, q] == k * n.half_blocks + b).astype(jnp.int32)
                hit = hit * (q < counts_b[r]).astype(jnp.int32)
                slot, live = slot + q * hit, live + hit
            chosen[b * B : (b + 1) * B, :] = kept(fb[slot], 0, live)

    def relay(w):
        def f(h, g):
            wait_recv(wholes[w // n.W].at[g, mine_blocks], xo_r.at[w, h])
            to_partner(w, h, g)

        at_owner(w, None, f)

    def gathered(w):
        for h in range(n.H):
            g = n.group(w, h)[0]
            wait_recv(wholes[w // n.W].at[g, other_blocks], wr_sem.at[w, h])

    def by_slot(dst, whole, rows, counts):
        for q in range(n.slots):
            for g in range(n.G):
                dst[q * B : (q + 1) * B, g * LANES : (g + 1) * LANES] = kept(
                    whole[g, rows[r, q]], q, counts[r]
                )

    group = (c * n.pw) // LANES
    inside = pl.multiple_of(lax.rem(c * n.pw, LANES), n.pw)

    def share(send, sem_s, sem_r, recv):
        recv[r] = send[r]
        for dr in range(1, n.R):
            to = lax.rem(r + dr, n.R)
            remote(send.at[to], recv.at[r], sem_s.at[dr - 1], sem_r.at[r], (to, c)).start()

    def add_up(recv, sem_s, sem_r, gather_s, gather_r, bag_ref):
        for dr in range(1, n.R):
            frm = lax.rem(r + dr, n.R)
            wait_recv(recv.at[frm], sem_r.at[frm])
        total = recv[0].astype(F32)
        for j in range(1, n.R):
            total = total + recv[j].astype(F32)
        spread(total, gather_s, gather_r, bag_ref)

    def spread(total, gather_s, gather_r, bag_ref):
        bag_ref[r] = total.astype(BF16)
        for dr in range(1, n.R):
            to = lax.rem(r + dr, n.R)
            remote(bag_ref.at[r], bag_ref.at[r], gather_s.at[dr - 1], gather_r.at[r], (to, c)).start()

    def gather_sums(bag_ref, gather_r):
        for dr in range(1, n.R):
            frm = lax.rem(r + dr, n.R)
            wait_recv(bag_ref.at[frm], gather_r.at[frm])

    def end_sends(send, sem_s):
        for dr in range(1, n.R):
            wait_recv(send.at[0], sem_s.at[dr - 1])

    def sums_a():
        for q in range(n.slots):
            at = slice(q * B, (q + 1) * B)
            part_a[at, :] = kept(whole_a[group, rows_a[r, q]], q, counts_a[r])
            part_c[at, :] = kept(whole_a[group, rows_b[r, q]], q, counts_b[r])
        for j, (left, right) in enumerate(((part_a[...], fa), (part_c[...], fb))):
            stage[...] = contract_rows(left, right[...].reshape(n.N, n.width))
            mine = stage[pl.ds(inside, n.pw), :]
            for i in range(n.R):
                ssend[i, j] = mine[i * n.rp : (i + 1) * n.rp].astype(BF16)
        share(ssend, rs_s, rs_r, srecv)

    def sums_a_add():
        add_up(srecv, rs_s, rs_r, ag_s.at[0], ag_r.at[0], agbuf)

    def tops():
        gather_sums(agbuf, ag_r.at[0])
        loads[3].wait()
        sum_a = jnp.concatenate([agbuf[i, 0] for i in range(n.R)], axis=0).astype(F32)
        sum_c = jnp.concatenate([agbuf[i, 1] for i in range(n.R)], axis=0).astype(F32)
        diag_a[...] = ba[...] - sum_a
        top[...] = (-(sum_c + times_exact(diag_a[...], ft[...]))).astype(BF16)
        copy_in(diag_a, diag_a_out, out_sem.at[1])
        copy_in(top, top_out, out_sem.at[2])
        for g in range(n.G):
            tsend[g] = top[:, g * LANES : (g + 1) * LANES]
        trecv[c] = tsend[group]
        for dc in range(1, n.C):
            to = lax.rem(c + dc, n.C)
            remote(
                tsend.at[(to * n.pw) // LANES], trecv.at[c], t_s.at[dc - 1], t_r.at[c], (r, to)
            ).start()

    def tops_in():
        for dc in range(1, n.C):
            frm = lax.rem(c + dc, n.C)
            wait_recv(trecv.at[frm], t_r.at[frm])
        columns = jnp.concatenate([trecv[i] for i in range(n.C)], axis=0)
        tt[...] = contract_rows(columns, ft[...])

    events = {}

    def after(t, f, *args):
        events.setdefault(min(t, end), []).append(functools.partial(f, *args))

    end = n.T + n.D
    last = n.chunks - 1
    for w in range(last):
        done = (w + 1) * n.per + n.D
        after(done, reduce_core, w)
        after(done + 1 * n.Q, reduce_x, w)
        after(done + 4 * n.Q, finish, w)
        if w < last - 1:
            after(done + 7 * n.Q, relay, w)
            after(done + 8 * n.Q, gathered, w)
    after(n.W * n.per + n.D + 8 * n.Q, sums_a)
    after(n.W * n.per + n.D + 2 * n.Q, choose)
    at = 0
    for t in sorted(set(events) | {n.D, end}):
        if t > at:
            segment(at, t)
            at = t
        if t == n.D:
            for cp in load_m:
                cp.wait()
        for f in events.get(t, ()):
            f()
    reduce_core(last)
    relay(last - 1)
    sums_a_add()
    reduce_x(last)
    tops()
    by_slot(slot_a, whole_a, rows_a, counts_a)
    copy_in(slot_a, col_a_out, out_sem.at[0])
    finish(last)
    for dr in range(n.R):
        frm = lax.rem(r + dr, n.R)
        for other in (1 - k, k)[: 2 if dr else 1]:
            wait_recv(brecv.at[frm, other], bs_r.at[frm, other])
    spread(sum(brecv[j, q].astype(F32) for j in range(n.R) for q in range(CORES)), ag_s.at[1], ag_r.at[1], bag)
    relay(last)
    tops_in()
    gathered(last - 1)
    gathered(last)
    by_slot(slot_b, whole_b, rows_b, counts_b)
    copy_in(slot_b, col_b_out, out_sem.at[3])
    for i in range(n.fanout):
        share_of = held.at[i]

        @pl.when(jnp.logical_and(trunk[i], jnp.logical_and(z >= z0[i], z < n.Z - 1)))
        def _():
            wait_recv(share_of, up_sem.at[i])

        @pl.when(jnp.logical_and(trunk[i], jnp.logical_and(z <= z0[i], z > 0)))
        def _():
            wait_recv(share_of, down_sem.at[i])

        @pl.when(trunk[i])
        def _():
            for dy in range(1, n.Y):
                wait_recv(share_of, y_sem.at[dy - 1, i])

    for w in range(n.chunks):
        wait_recv(s1.at[w], core_s.at[w])

        def sent(h, g):
            for dx in range(1, n.X):
                wait_recv(x2s.at[w, h], xo_s.at[w, h, dx - 1])
            for c_to in n.columns(g) if w >= n.W else ():
                for dr, kd, to, copy in to_owners(w % n.W, c_to):
                    if dr:
                        copy.wait_send()
                    else:
                        pl.when(k != kd)(copy.wait_send)

        def sent_part(h, g):
            wait_recv(x2s.at[w, h], xs_sem.at[w, h])

        at_owner(w, sent, sent_part)
        for h in range(n.H):
            wait_recv(x2s.at[w, h], ws_sem.at[w, h])
    for dc in range(1, n.C):
        wait_recv(tsend.at[0], t_s.at[dc - 1])
    loads[4].wait()
    gather_sums(bag, ag_r.at[1])
    sum_b = jnp.concatenate([bag[i] for i in range(n.R)], axis=0).astype(F32)
    diag_b[...] = bb[...] - sum_b - tt[pl.ds(inside, n.pw), :]
    copy_in(diag_b, diag_b_out, out_sem.at[4])
    end_sends(ssend, rs_s)
    end_sends(agbuf, ag_s.at[0])
    end_sends(bag, ag_s.at[1])
    for j, (a, b) in enumerate(
        (
            (slot_a, col_a_out),
            (diag_a, diag_a_out),
            (top, top_out),
            (slot_b, col_b_out),
            (diag_b, diag_b_out),
        )
    ):
        pltpu.make_async_copy(a, b, out_sem.at[j]).wait()


def hand_over(*refs):
    count = (len(refs) - 2) // 3
    sources, results, held = (refs[j * count : (j + 1) * count] for j in range(3))
    load_sem, store_sem = refs[-2:]
    loads = [
        pltpu.make_async_copy(a, b, load_sem.at[j]) for j, (a, b) in enumerate(zip(sources, held))
    ]
    stores = [
        pltpu.make_async_copy(a, b, store_sem.at[j]) for j, (a, b) in enumerate(zip(held, results))
    ]
    for cp in loads:
        cp.start()
    for load, store in zip(loads, stores):
        load.wait()
        store.start()
    for cp in stores:
        cp.wait()


def handed_over(arrays):
    spec = pl.BlockSpec(memory_space=pl.ANY)
    count = len(arrays)
    return pl.pallas_call(
        hand_over,
        out_shape=tuple(jax.ShapeDtypeStruct(a.shape, a.dtype) for a in arrays),
        in_specs=[spec] * count,
        out_specs=(spec,) * count,
        scratch_shapes=[pltpu.VMEM(a.shape, a.dtype) for a in arrays]
        + [pltpu.SemaphoreType.DMA((count,))] * 2,
        compiler_params=pltpu.CompilerParams(vmem_limit_bytes=60 << 20),
    )(*arrays)


def solution(mesh):
    R, C = mesh.shape["row"], mesh.shape["col"]

    def on_device(trailing, rows_a, counts_a, factor_a, rows_b, counts_b, factor_b, factor_top, base_a, base_b):
        n = Sizes(R, C, trailing.shape, rows_a.shape, factor_a.shape)
        any_ = pl.BlockSpec(memory_space=pl.ANY)
        smem = pl.BlockSpec(memory_space=pltpu.SMEM)
        vm = pltpu.VMEM
        blocks = (n.row_blocks, n.block, LANES)
        dma = pltpu.SemaphoreType.DMA
        shape = jax.ShapeDtypeStruct
        scratch = [
            vm((n.mcols // n.block, n.mrows, n.block), BF16),
            vm((n.slots * PARTS, n.piece, n.width), BF16),
            vm((n.slots * PARTS, n.piece, n.width), BF16),
            vm(factor_top.shape, BF16),
            vm(base_a.shape, F32),
            vm(base_b.shape, F32),
            vm((n.fanout, n.T, n.piece, n.cw), BF16),
            vm((n.fanout * n.deep * n.block, n.cw), BF16),
            vm((n.mrows, n.cw), F32),
            vm((n.half, n.cw), F32),
            vm((n.chunks, n.half, n.cw), BF16),
            vm((n.chunks, n.half, n.cw), BF16),
            vm((n.chunks, n.H, n.half, LANES), BF16),
            vm((n.chunks, n.H, n.X, n.half, LANES), BF16),
            vm((n.G,) + blocks, BF16),
            vm((n.G,) + blocks, BF16),
            vm((n.half, n.width), BF16),
            vm(factor_a.shape, BF16),
            vm(factor_b.shape, BF16),
            vm((n.N, LANES), BF16),
            vm((n.N, LANES), BF16),
            vm((LANES, n.width), F32),
            vm((n.R, 2, n.rp, n.width), BF16),
            vm((n.R, 2, n.rp, n.width), BF16),
            vm((n.R, 2, n.rp, n.width), BF16),
            vm((n.W, CORES, n.R, n.rp, n.width), BF16),
            vm((n.R, CORES, n.rp, n.width), BF16),
            vm((n.R, n.rp, n.width), BF16),
            vm((n.pw, n.width), F32),
            vm((n.pw, n.width), BF16),
            vm((n.G, n.pw, LANES), BF16),
            vm((n.C, n.pw, LANES), BF16),
            vm((LANES, n.width), F32),
            vm((n.pw, n.width), F32),
            dma((6,)),
            dma((n.mcols // n.block,)),
            dma((n.chunks, n.H)),
            dma((n.fanout, n.T)),
            dma((n.fanout,)),
            dma((n.fanout,)),
            dma((n.Y - 1, n.fanout)),
            dma((n.chunks,)),
            dma((n.chunks,)),
            dma((n.chunks, n.H)),
            dma((n.chunks, n.H, n.X)),
            dma((n.chunks, n.H, n.X - 1)),
            dma((n.chunks, n.H)),
            dma((n.chunks, n.H)),
            dma((n.chunks, n.H)),
            dma((n.R - 1,)),
            dma((n.R,)),
            dma((n.W, CORES, n.R)),
            dma((n.R, CORES)),
            dma((2, n.R - 1)),
            dma((2, n.R)),
            dma((n.C - 1,)),
            dma((n.C,)),
            dma((5,)),
        ]
        results = pl.pallas_call(
            functools.partial(kernel, n),
            out_shape=(
                shape(factor_a.shape, BF16),
                shape((n.pw, n.width), F32),
                shape(factor_b.shape, BF16),
                shape((n.pw, n.width), BF16),
                shape((n.pw, n.width), F32),
            ),
            in_specs=[any_, smem, smem, any_, smem, smem, any_, any_, any_, any_],
            out_specs=(any_,) * 5,
            scratch_shapes=scratch,
            compiler_params=pltpu.CompilerParams(
                collective_id=0, has_side_effects=True, vmem_limit_bytes=60 << 20
            ),
        )(
            trailing,
            rows_a,
            counts_a,
            factor_a.reshape(n.slots * PARTS, n.piece, n.width),
            rows_b,
            counts_b,
            factor_b.reshape(n.slots * PARTS, n.piece, n.width),
            factor_top,
            base_a,
            base_b,
        )
        return handed_over(results)

    in_specs = (
        P("row", "col"),
        P(),
        P(),
        P("row", None),
        P(),
        P(),
        P("row", None),
        P(),
        P("col", None),
        P("col", None),
    )
    out_specs = (P("row", None), P("col", None), P("row", None), P("col", None), P("col", None))
    return jax.shard_map(
        on_device, mesh=mesh, in_specs=in_specs, out_specs=out_specs, check_vma=False
    )
```

```python
import functools

import jax
import jax.numpy as jnp
from jax import lax
from jax.experimental import pallas as pl
from jax.experimental.pallas import tpu as pltpu
from jax.sharding import PartitionSpec as P

MESH = pl.DeviceIdType.MESH
LANES = 128
CORES = 2
PARTS = 1
SKEW = 4
CROSS = 3
F32 = jnp.float32
BF16 = jnp.bfloat16


def contract_rows(former, latter):
    return lax.dot_general(
        former, latter, (((0,), (0,)), ((), ())), preferred_element_type=F32
    )


def times_exact(left, right):
    total = None
    for _ in range(3):
        term = left.astype(BF16)
        left = left - term.astype(F32)
        product = jnp.dot(term, right, preferred_element_type=F32)
        total = product if total is None else total + product
    return total


def kept(value, position, count):
    counts = jnp.full((1, value.shape[-1]), count, jnp.int32)
    return value * jnp.where(counts > position, 1.0, 0.0).astype(value.dtype)


class Sizes:
    def __init__(self, rows, cols, trailing, table, factor):
        self.R, self.C = rows, cols
        self.fanout = rows // cols
        self.slots = table[1]
        self.N, self.width = factor
        self.block = self.N // self.slots
        self.mrows, self.mcols = trailing
        self.row_blocks = self.mrows // self.block
        self.X = cols // CORES
        self.Y = self.X
        while rows % self.Y:
            self.Y -= 1
        self.Z = rows // self.Y
        self.deep = 2 - self.slots % 2
        self.cw = CORES * LANES
        self.W = self.width // self.cw
        self.chunks = 2 * self.W
        self.per = self.slots * PARTS
        self.Q = self.deep * PARTS
        self.T = self.chunks * self.per
        self.piece = self.block // PARTS
        self.D = SKEW * (self.Z - 1) + CROSS
        self.pw = self.width // cols
        self.rp = self.pw // rows
        self.tile = self.mrows
        while self.tile > 512:
            self.tile //= 2
        self.G = self.width // LANES
        self.H = self.cw // LANES
        self.half = self.mrows // CORES
        self.half_blocks = self.row_blocks // CORES
        self.htile = self.half // 2

    def group(self, w, h):
        g = w % self.W + self.W * h
        return g, g * LANES // (self.pw * CORES)

    def columns(self, g):
        return [c for c in range(self.C) if c * self.pw // LANES == g]


def kernel(n, *refs):
    (
        m_hbm, rows_a, counts_a, fa_hbm, rows_b, counts_b, fb_hbm, ft_hbm, ba_hbm, bb_hbm,
        col_a_out, diag_a_out, col_b_out, top_out, diag_b_out,
        m, fa, fb, ft, ba, bb, held, rhs, acc, own, s1, r1, x2s, x2r, whole_a, whole_b, chosen,
        slot_a, slot_b, part_a, part_c, stage, ssend, srecv, agbuf, bsend, brecv, bag,
        diag_a, top, tsend, trecv, tt, diag_b,
        in_sem, m_sem, src_sem, lane_sem, up_sem, down_sem, y_sem,
        core_s, core_r, xs_sem, xr_sem, xo_s, xo_r, ws_sem, wr_sem,
        rs_s, rs_r, bs_s, bs_r, ag_s, ag_r, t_s, t_r, out_sem,
    ) = refs
    B = n.block
    r, c = lax.axis_index("row"), lax.axis_index("col")
    z, y = r // n.Y, r % n.Y
    x, k = c // CORES, c % CORES
    owners = [c + n.C * i for i in range(n.fanout)]
    z0 = [o // n.Y for o in owners]
    y0 = [o % n.Y for o in owners]
    src = [r == o for o in owners]
    hop = [jnp.abs(z - q) for q in z0]

    def copy_in(a, b, sem):
        cp = pltpu.make_async_copy(a, b, sem)
        cp.start()
        return cp

    def remote(a, b, s, d, dev):
        return pltpu.make_async_remote_copy(
            src_ref=a, dst_ref=b, send_sem=s, recv_sem=d, device_id=dev, device_id_type=MESH
        )

    def wait_recv(ref, sem):
        pltpu.make_async_copy(ref, ref, sem).wait()

    def source_copies(i):
        for w in range(n.chunks):
            whole = (fa_hbm, fb_hbm)[w // n.W]
            for h in range(n.H):
                yield pltpu.make_async_copy(
                    whole.at[:, :, pl.ds(n.group(w, h)[0] * LANES, LANES)],
                    held.at[i, pl.ds(w * n.per, n.per), :, pl.ds(h * LANES, LANES)],
                    src_sem.at[w, h],
                )

    for i in range(n.fanout):

        @pl.when(src[i])
        def _():
            for cp in source_copies(i):
                cp.start()

    load_m = [
        copy_in(m_hbm.at[:, j * B : (j + 1) * B], m.at[j], m_sem.at[j])
        for j in range(n.mcols // B)
    ]
    loads = [
        copy_in(a, b, in_sem.at[1 + j])
        for j, (a, b) in enumerate(
            ((fa_hbm, fa), (fb_hbm, fb), (ft_hbm, ft), (ba_hbm, ba), (bb_hbm, bb))
        )
    ]

    barrier = pltpu.get_barrier_semaphore()
    peers = [(lax.rem(r + dr, n.R), c) for dr in range(1, n.R)]
    peers += [(r, lax.rem(c + dc, n.C)) for dc in range(1, n.C)]
    for dev in peers:
        pl.semaphore_signal(barrier, inc=1, device_id=dev, device_id_type=MESH)
    pl.semaphore_wait(barrier, len(peers))
    for i in range(n.fanout):

        @pl.when(src[i])
        def _():
            for cp in source_copies(i):
                cp.wait()

    trunk = [y == q for q in y0]

    def forward(i, t):
        u = t - SKEW * hop[i]

        @pl.when(jnp.logical_and(trunk[i], jnp.logical_and(u >= 0, u < n.T)))
        def _():
            piece = held.at[i, u]

            @pl.when(jnp.logical_not(src[i]))
            def _():
                wait_recv(piece, lane_sem.at[i, u])

            @pl.when(jnp.logical_and(z >= z0[i], z < n.Z - 1))
            def _():
                remote(piece, piece, up_sem.at[i], lane_sem.at[i, u], (r + n.Y, c)).start()

            @pl.when(jnp.logical_and(z <= z0[i], z > 0))
            def _():
                remote(piece, piece, down_sem.at[i], lane_sem.at[i, u], (r - n.Y, c)).start()

            for dy in range(1, n.Y):
                dev = (z * n.Y + lax.rem(y + dy, n.Y), c)
                remote(piece, piece, y_sem.at[dy - 1, i], lane_sem.at[i, u], dev).start()

    def product(v):
        s = lax.rem(v, n.slots // n.deep)
        first = v < n.W * (n.slots // n.deep)
        cols = []
        for i in range(n.fanout):

            @pl.when(jnp.logical_not(trunk[i]))
            def _():
                for h in range(n.Q):
                    u = v * n.Q + h
                    wait_recv(held.at[i, u], lane_sem.at[i, u])

        for i in range(n.fanout):
            count = jnp.where(first, counts_a[owners[i]], counts_b[owners[i]])
            for j in range(n.deep):
                q = s * n.deep + j
                row = jnp.where(first, rows_a[owners[i], q], rows_b[owners[i], q])
                block = held[i, pl.ds(v * n.Q + j * PARTS, PARTS)].reshape(B, n.cw)
                rhs[len(cols) * B : (len(cols) + 1) * B, :] = kept(block, q, count)
                cols.append(row * n.fanout + i)

        @pl.loop(0, n.mrows // n.tile)
        def _(step):
            at = pl.ds(pl.multiple_of(step * n.tile, n.tile), n.tile)
            left = jnp.concatenate([m[col, at, :] for col in cols], axis=1)
            part = jnp.dot(left, rhs[...], preferred_element_type=F32)

            @pl.when(s == 0)
            def _():
                acc[at, :] = part

            @pl.when(s != 0)
            def _():
                acc[at, :] += part

    def segment(start, stop):
        def body(t, carry):
            for i in range(n.fanout):
                forward(i, t)
            late = t - n.D + 1

            @pl.when(jnp.logical_and(late > 0, lax.rem(late, n.Q) == 0))
            def _():
                product(lax.div(late, n.Q) - 1)

            return carry

        lax.fori_loop(start, stop, body, 0)

    partner = (r, c + 1 - 2 * k)

    mine_rows = pl.ds(pl.multiple_of(k * n.half, n.half), n.half)
    mine_blocks = pl.ds(k * n.half_blocks, n.half_blocks)
    other_blocks = pl.ds((1 - k) * n.half_blocks, n.half_blocks)
    wholes = (whole_a, whole_b)

    def half_tiles(f):
        @pl.loop(0, n.half // n.htile)
        def _(step):
            f(pl.multiple_of(step * n.htile, n.htile))

    def at_owner(w, f, g=None):
        for h in range(n.H):
            index, chip = n.group(w, h)
            if f is not None:

                @pl.when(x == chip)
                def _():
                    f(h, index)

            if g is not None:

                @pl.when(x != chip)
                def _():
                    g(h, index)

    def reduce_core(w):
        def f(at):
            theirs = pl.ds(pl.multiple_of((1 - k) * n.half + at, n.htile), n.htile)
            ours = pl.ds(pl.multiple_of(k * n.half + at, n.htile), n.htile)
            s1[w, pl.ds(at, n.htile), :] = acc[theirs, :].astype(BF16)
            part = s1.at[w, pl.ds(at, n.htile)]
            step = lax.div(at, n.htile)
            remote(
                part, r1.at[w, pl.ds(at, n.htile)], core_s.at[w, step], core_r.at[w, step], partner
            ).start()
            own[pl.ds(at, n.htile), :] = acc[ours, :]

        half_tiles(f)

    def reduce_x(w):
        def f(at):
            rows = pl.ds(at, n.htile)
            step = lax.div(at, n.htile)
            wait_recv(r1.at[w, rows], core_r.at[w, step])
            total = own[rows, :] + r1[w, rows, :].astype(F32)
            own[rows, :] = total
            for h in range(n.H):
                x2s[w, h, rows, :] = total[:, h * LANES : (h + 1) * LANES].astype(BF16)

            def send(h, g):
                remote(
                    x2s.at[w, h, rows],
                    x2r.at[w, h, x, rows],
                    xs_sem.at[w, h, step],
                    xr_sem.at[w, h, x, step],
                    (r, n.group(w, h)[1] * CORES + k),
                ).start()

            at_owner(w, None, send)

        half_tiles(f)

    def to_partner(w, h, g):
        part = wholes[w // n.W].at[g, mine_blocks]
        remote(part, part, ws_sem.at[w, h], wr_sem.at[w, h], partner).start()

    def finish(w):
        node = w // n.W

        def own_group(h, g):
            def f(at):
                rows = pl.ds(at, n.htile)
                for dx in range(1, n.X):
                    frm = lax.rem(x + dx, n.X)
                    wait_recv(x2r.at[w, h, frm, rows], xr_sem.at[w, h, frm, lax.div(at, n.htile)])
                count = n.htile // B
                some = pl.ds(k * n.half_blocks + lax.div(at, B), count)
                total = own[rows, h * LANES : (h + 1) * LANES]
                for dx in range(1, n.X):
                    total = total + x2r[w, h, lax.rem(x + dx, n.X), rows, :].astype(F32)
                if node:
                    left = jnp.concatenate(
                        [whole_a[j, some].reshape(n.htile, LANES) for j in range(n.G)], axis=1
                    )
                    right = ft[:, g * LANES : (g + 1) * LANES]
                    total = total + jnp.dot(left, right, preferred_element_type=F32)
                value = (-total).astype(BF16).reshape(count, B, LANES)
                wholes[node][g, some] = value

            half_tiles(f)
            part = wholes[node].at[g, mine_blocks]
            for dx in range(1, n.X):
                to = lax.rem(x + dx, n.X)
                remote(
                    part, part, xo_s.at[w, h, dx - 1], xo_r.at[w, h], (r, to * CORES + k)
                ).start()
            to_partner(w, h, g)
            if node:
                sums_b(w % n.W, g)

        at_owner(w, own_group)

    def to_owners(turn, c_to):
        kd = c_to % CORES
        for dr in range(n.R):
            to = lax.rem(r + dr, n.R)
            copy = remote(
                bsend.at[turn, kd, to], brecv.at[r, k], bs_s.at[turn, kd, dr], bs_r.at[r, k], (to, c_to)
            )
            yield dr, kd, to, copy

    def sums_b(turn, g):
        left = whole_b[g, mine_blocks].reshape(n.half, LANES)
        sums = contract_rows(left, chosen[...])
        for c_to in n.columns(g):
            inside = c_to * n.pw - g * LANES
            kd = c_to % CORES
            for i in range(n.R):
                at = inside + i * n.rp
                bsend[turn, kd, i] = sums[at : at + n.rp].astype(BF16)
            for dr, kd, to, copy in to_owners(turn, c_to):
                if dr:
                    copy.start()
                else:
                    pl.when(k != kd)(copy.start)

                    @pl.when(k == kd)
                    def _():
                        brecv[r, k] = bsend[turn, kd, to]

    def choose():
        for cp in loads[:3]:
            cp.wait()
        for b in range(n.half_blocks):
            slot, live = 0, 0
            for q in range(n.slots):
                hit = (rows_b[r, q] == k * n.half_blocks + b).astype(jnp.int32)
                hit = hit * (q < counts_b[r]).astype(jnp.int32)
                slot, live = slot + q * hit, live + hit
            chosen[b * B : (b + 1) * B, :] = kept(fb[slot], 0, live)

    def relay(w):
        def f(h, g):
            wait_recv(wholes[w // n.W].at[g, mine_blocks], xo_r.at[w, h])
            to_partner(w, h, g)

        at_owner(w, None, f)

    def gathered(w):
        for h in range(n.H):
            g = n.group(w, h)[0]
            wait_recv(wholes[w // n.W].at[g, other_blocks], wr_sem.at[w, h])

    def by_slot(dst, whole, rows, counts):
        for q in range(n.slots):
            for g in range(n.G):
                dst[q * B : (q + 1) * B, g * LANES : (g + 1) * LANES] = kept(
                    whole[g, rows[r, q]], q, counts[r]
                )

    group = (c * n.pw) // LANES
    inside = pl.multiple_of(lax.rem(c * n.pw, LANES), n.pw)

    def share(send, sem_s, sem_r, recv):
        recv[r] = send[r]
        for dr in range(1, n.R):
            to = lax.rem(r + dr, n.R)
            remote(send.at[to], recv.at[r], sem_s.at[dr - 1], sem_r.at[r], (to, c)).start()

    def add_up(recv, sem_s, sem_r, gather_s, gather_r, bag_ref):
        for dr in range(1, n.R):
            frm = lax.rem(r + dr, n.R)
            wait_recv(recv.at[frm], sem_r.at[frm])
        total = recv[0].astype(F32)
        for j in range(1, n.R):
            total = total + recv[j].astype(F32)
        spread(total, gather_s, gather_r, bag_ref)

    def spread(total, gather_s, gather_r, bag_ref):
        bag_ref[r] = total.astype(BF16)
        for dr in range(1, n.R):
            to = lax.rem(r + dr, n.R)
            remote(bag_ref.at[r], bag_ref.at[r], gather_s.at[dr - 1], gather_r.at[r], (to, c)).start()

    def gather_sums(bag_ref, gather_r):
        for dr in range(1, n.R):
            frm = lax.rem(r + dr, n.R)
            wait_recv(bag_ref.at[frm], gather_r.at[frm])

    def end_sends(send, sem_s):
        for dr in range(1, n.R):
            wait_recv(send.at[0], sem_s.at[dr - 1])

    def sums_a():
        for q in range(n.slots):
            at = slice(q * B, (q + 1) * B)
            part_a[at, :] = kept(whole_a[group, rows_a[r, q]], q, counts_a[r])
            part_c[at, :] = kept(whole_a[group, rows_b[r, q]], q, counts_b[r])
        for j, (left, right) in enumerate(((part_a[...], fa), (part_c[...], fb))):
            stage[...] = contract_rows(left, right[...].reshape(n.N, n.width))
            mine = stage[pl.ds(inside, n.pw), :]
            for i in range(n.R):
                ssend[i, j] = mine[i * n.rp : (i + 1) * n.rp].astype(BF16)
        share(ssend, rs_s, rs_r, srecv)

    def sums_a_add():
        add_up(srecv, rs_s, rs_r, ag_s.at[0], ag_r.at[0], agbuf)

    def tops():
        gather_sums(agbuf, ag_r.at[0])
        loads[3].wait()
        sum_a = jnp.concatenate([agbuf[i, 0] for i in range(n.R)], axis=0).astype(F32)
        sum_c = jnp.concatenate([agbuf[i, 1] for i in range(n.R)], axis=0).astype(F32)
        diag_a[...] = ba[...] - sum_a
        top[...] = (-(sum_c + times_exact(diag_a[...], ft[...]))).astype(BF16)
        copy_in(diag_a, diag_a_out, out_sem.at[1])
        copy_in(top, top_out, out_sem.at[2])
        for g in range(n.G):
            tsend[g] = top[:, g * LANES : (g + 1) * LANES]
        trecv[c] = tsend[group]
        for dc in range(1, n.C):
            to = lax.rem(c + dc, n.C)
            remote(
                tsend.at[(to * n.pw) // LANES], trecv.at[c], t_s.at[dc - 1], t_r.at[c], (r, to)
            ).start()

    def tops_in():
        for dc in range(1, n.C):
            frm = lax.rem(c + dc, n.C)
            wait_recv(trecv.at[frm], t_r.at[frm])
        columns = jnp.concatenate([trecv[i] for i in range(n.C)], axis=0)
        tt[...] = contract_rows(columns, ft[...])

    events = {}

    def after(t, f, *args):
        events.setdefault(min(t, end), []).append(functools.partial(f, *args))

    end = n.T + n.D
    last = n.chunks - 1
    for w in range(last):
        done = (w + 1) * n.per + n.D
        after(done, reduce_core, w)
        after(done + 1 * n.Q, reduce_x, w)
        after(done + 4 * n.Q, finish, w)
        if w < last - 1:
            after(done + 7 * n.Q, relay, w)
            after(done + 8 * n.Q, gathered, w)
    after(n.W * n.per + n.D + 8 * n.Q, sums_a)
    after(n.W * n.per + n.D + 2 * n.Q, choose)
    at = 0
    for t in sorted(set(events) | {n.D, end}):
        if t > at:
            segment(at, t)
            at = t
        if t == n.D:
            for cp in load_m:
                cp.wait()
        for f in events.get(t, ()):
            f()
    reduce_core(last)
    relay(last - 1)
    sums_a_add()
    reduce_x(last)
    tops()
    by_slot(slot_a, whole_a, rows_a, counts_a)
    copy_in(slot_a, col_a_out, out_sem.at[0])
    finish(last)
    for dr in range(n.R):
        frm = lax.rem(r + dr, n.R)
        for other in (1 - k, k)[: 2 if dr else 1]:
            wait_recv(brecv.at[frm, other], bs_r.at[frm, other])
    spread(sum(brecv[j, q].astype(F32) for j in range(n.R) for q in range(CORES)), ag_s.at[1], ag_r.at[1], bag)
    relay(last)
    tops_in()
    gathered(last - 1)
    gathered(last)
    by_slot(slot_b, whole_b, rows_b, counts_b)
    copy_in(slot_b, col_b_out, out_sem.at[3])
    for i in range(n.fanout):
        share_of = held.at[i]

        @pl.when(jnp.logical_and(trunk[i], jnp.logical_and(z >= z0[i], z < n.Z - 1)))
        def _():
            wait_recv(share_of, up_sem.at[i])

        @pl.when(jnp.logical_and(trunk[i], jnp.logical_and(z <= z0[i], z > 0)))
        def _():
            wait_recv(share_of, down_sem.at[i])

        @pl.when(trunk[i])
        def _():
            for dy in range(1, n.Y):
                wait_recv(share_of, y_sem.at[dy - 1, i])

    for w in range(n.chunks):
        for step in range(n.half // n.htile):
            wait_recv(s1.at[w, pl.ds(0, n.htile)], core_s.at[w, step])

        def sent(h, g):
            for dx in range(1, n.X):
                wait_recv(x2s.at[w, h], xo_s.at[w, h, dx - 1])
            for c_to in n.columns(g) if w >= n.W else ():
                for dr, kd, to, copy in to_owners(w % n.W, c_to):
                    if dr:
                        copy.wait_send()
                    else:
                        pl.when(k != kd)(copy.wait_send)

        def sent_part(h, g):
            for step in range(n.half // n.htile):
                wait_recv(x2s.at[w, h, pl.ds(0, n.htile)], xs_sem.at[w, h, step])

        at_owner(w, sent, sent_part)
        for h in range(n.H):
            wait_recv(x2s.at[w, h], ws_sem.at[w, h])
    for dc in range(1, n.C):
        wait_recv(tsend.at[0], t_s.at[dc - 1])
    loads[4].wait()
    gather_sums(bag, ag_r.at[1])
    sum_b = jnp.concatenate([bag[i] for i in range(n.R)], axis=0).astype(F32)
    diag_b[...] = bb[...] - sum_b - tt[pl.ds(inside, n.pw), :]
    copy_in(diag_b, diag_b_out, out_sem.at[4])
    end_sends(ssend, rs_s)
    end_sends(agbuf, ag_s.at[0])
    end_sends(bag, ag_s.at[1])
    for j, (a, b) in enumerate(
        (
            (slot_a, col_a_out),
            (diag_a, diag_a_out),
            (top, top_out),
            (slot_b, col_b_out),
            (diag_b, diag_b_out),
        )
    ):
        pltpu.make_async_copy(a, b, out_sem.at[j]).wait()


def hand_over(*refs):
    count = (len(refs) - 2) // 3
    sources, results, held = (refs[j * count : (j + 1) * count] for j in range(3))
    load_sem, store_sem = refs[-2:]
    loads = [
        pltpu.make_async_copy(a, b, load_sem.at[j]) for j, (a, b) in enumerate(zip(sources, held))
    ]
    stores = [
        pltpu.make_async_copy(a, b, store_sem.at[j]) for j, (a, b) in enumerate(zip(held, results))
    ]
    for cp in loads:
        cp.start()
    for load, store in zip(loads, stores):
        load.wait()
        store.start()
    for cp in stores:
        cp.wait()


def handed_over(arrays):
    spec = pl.BlockSpec(memory_space=pl.ANY)
    count = len(arrays)
    return pl.pallas_call(
        hand_over,
        out_shape=tuple(jax.ShapeDtypeStruct(a.shape, a.dtype) for a in arrays),
        in_specs=[spec] * count,
        out_specs=(spec,) * count,
        scratch_shapes=[pltpu.VMEM(a.shape, a.dtype) for a in arrays]
        + [pltpu.SemaphoreType.DMA((count,))] * 2,
        compiler_params=pltpu.CompilerParams(vmem_limit_bytes=60 << 20),
    )(*arrays)


def solution(mesh):
    R, C = mesh.shape["row"], mesh.shape["col"]

    def on_device(trailing, rows_a, counts_a, factor_a, rows_b, counts_b, factor_b, factor_top, base_a, base_b):
        n = Sizes(R, C, trailing.shape, rows_a.shape, factor_a.shape)
        any_ = pl.BlockSpec(memory_space=pl.ANY)
        smem = pl.BlockSpec(memory_space=pltpu.SMEM)
        vm = pltpu.VMEM
        blocks = (n.row_blocks, n.block, LANES)
        dma = pltpu.SemaphoreType.DMA
        shape = jax.ShapeDtypeStruct
        scratch = [
            vm((n.mcols // n.block, n.mrows, n.block), BF16),
            vm((n.slots * PARTS, n.piece, n.width), BF16),
            vm((n.slots * PARTS, n.piece, n.width), BF16),
            vm(factor_top.shape, BF16),
            vm(base_a.shape, F32),
            vm(base_b.shape, F32),
            vm((n.fanout, n.T, n.piece, n.cw), BF16),
            vm((n.fanout * n.deep * n.block, n.cw), BF16),
            vm((n.mrows, n.cw), F32),
            vm((n.half, n.cw), F32),
            vm((n.chunks, n.half, n.cw), BF16),
            vm((n.chunks, n.half, n.cw), BF16),
            vm((n.chunks, n.H, n.half, LANES), BF16),
            vm((n.chunks, n.H, n.X, n.half, LANES), BF16),
            vm((n.G,) + blocks, BF16),
            vm((n.G,) + blocks, BF16),
            vm((n.half, n.width), BF16),
            vm(factor_a.shape, BF16),
            vm(factor_b.shape, BF16),
            vm((n.N, LANES), BF16),
            vm((n.N, LANES), BF16),
            vm((LANES, n.width), F32),
            vm((n.R, 2, n.rp, n.width), BF16),
            vm((n.R, 2, n.rp, n.width), BF16),
            vm((n.R, 2, n.rp, n.width), BF16),
            vm((n.W, CORES, n.R, n.rp, n.width), BF16),
            vm((n.R, CORES, n.rp, n.width), BF16),
            vm((n.R, n.rp, n.width), BF16),
            vm((n.pw, n.width), F32),
            vm((n.pw, n.width), BF16),
            vm((n.G, n.pw, LANES), BF16),
            vm((n.C, n.pw, LANES), BF16),
            vm((LANES, n.width), F32),
            vm((n.pw, n.width), F32),
            dma((6,)),
            dma((n.mcols // n.block,)),
            dma((n.chunks, n.H)),
            dma((n.fanout, n.T)),
            dma((n.fanout,)),
            dma((n.fanout,)),
            dma((n.Y - 1, n.fanout)),
            dma((n.chunks, n.half // n.htile)),
            dma((n.chunks, n.half // n.htile)),
            dma((n.chunks, n.H, n.half // n.htile)),
            dma((n.chunks, n.H, n.X, n.half // n.htile)),
            dma((n.chunks, n.H, n.X - 1)),
            dma((n.chunks, n.H)),
            dma((n.chunks, n.H)),
            dma((n.chunks, n.H)),
            dma((n.R - 1,)),
            dma((n.R,)),
            dma((n.W, CORES, n.R)),
            dma((n.R, CORES)),
            dma((2, n.R - 1)),
            dma((2, n.R)),
            dma((n.C - 1,)),
            dma((n.C,)),
            dma((5,)),
        ]
        results = pl.pallas_call(
            functools.partial(kernel, n),
            out_shape=(
                shape(factor_a.shape, BF16),
                shape((n.pw, n.width), F32),
                shape(factor_b.shape, BF16),
                shape((n.pw, n.width), BF16),
                shape((n.pw, n.width), F32),
            ),
            in_specs=[any_, smem, smem, any_, smem, smem, any_, any_, any_, any_],
            out_specs=(any_,) * 5,
            scratch_shapes=scratch,
            compiler_params=pltpu.CompilerParams(
                collective_id=0, has_side_effects=True, vmem_limit_bytes=60 << 20
            ),
        )(
            trailing,
            rows_a,
            counts_a,
            factor_a.reshape(n.slots * PARTS, n.piece, n.width),
            rows_b,
            counts_b,
            factor_b.reshape(n.slots * PARTS, n.piece, n.width),
            factor_top,
            base_a,
            base_b,
        )
        return handed_over(results)

    in_specs = (
        P("row", "col"),
        P(),
        P(),
        P("row", None),
        P(),
        P(),
        P("row", None),
        P(),
        P("col", None),
        P("col", None),
    )
    out_specs = (P("row", None), P("col", None), P("row", None), P("col", None), P("col", None))
    return jax.shard_map(
        on_device, mesh=mesh, in_specs=in_specs, out_specs=out_specs, check_vma=False
    )
```
